32 devices in a mesh: dp: 16 (over z, y, core), ctx: 2 (over x).
Axes of the slice: x: 2, y: 2, z: 4, core: 2. Of those that a mesh axis runs over, the one named last changes fastest.
Arguments:
- tokens: bfloat16 [16384, 768], P(('dp', 'ctx')), may hold values from -6 to 6
- out_grad: bfloat16 [16384, 768], P(('dp', 'ctx')), may hold values from -6 to 6
- segments: int32 [16384], P(('dp', 'ctx')), may hold values from 0 to 3, as said below
- positions: int32 [16384], P(('dp', 'ctx')), may hold values from 0 to 717, as said below
- params: float32 [32, 221472], P(('dp', 'ctx')), may hold values from -3 to 3
- first_moment: float32 [32, 221472], P(('dp', 'ctx')), may hold values from -0.0009765625 to 0.0009765625
- second_moment: float32 [32, 221472], P(('dp', 'ctx')), may hold values from 3.6686354e-09 to 2.9631286e-08
Outputs:
- result: bfloat16 [16384, 768], P(('dp', 'ctx'))
- input_grad: float32 [16384, 768], P(('dp', 'ctx'))
- grads: float32 [32, 221472], P(('dp', 'ctx'))
- new_params: float32 [32, 221472], P(('dp', 'ctx'))
- new_first: float32 [32, 221472], P(('dp', 'ctx'))
- new_second: float32 [32, 221472], P(('dp', 'ctx'))
The draws below stay inside these ranges and needn't reach their ends.
Inputs may be any that keep to these rules, and one draw needn't show every extreme that they name: `segments`: within each sequence of 1024 tokens the segment numbers start at 0, never fall, and count exactly 4 documents. `positions`: each token's position is its distance from the first token of its document.
All inputs are finite; a program needn't handle non-finite values.
Results may differ from the reference program's by a relative error of at most 0.0087.
The reference program's roundings to bfloat16 on the way count: a program that leaves them out, or rounds other values in their place, can miss the bound.
Values may be sent and summed in bfloat16 or wider, within the bound.
No kernel may reach another device: no remote copies, remote signals or barrier semaphores. Data moves between devices by JAX's collectives and lax.ppermute only.
A program may use at most 192 MiB of HBM per device.

```python
import math
import jax
import jax.numpy as jnp
from jax import lax

D = 768
HEADS = 12
HEAD_DIM = 64
ROT = 16
FF = 3072
SEQ_LEN = 1024
SEQS = 16
OWNERS = 32
TOKENS = 16384
NPARAM = 7087104
PARAM_DEV = 221472


def document_layout(key):
    lengths = jax.random.randint(jax.random.fold_in(key, 11), (SEQS, 3), SEQ_LEN // 10, 3 * SEQ_LEN // 10 + 1)
    chosen = jax.random.randint(jax.random.fold_in(key, 12), (), 0, SEQS)
    pick_row = (jnp.arange(SEQS, dtype=jnp.int32) == chosen)[:, None]
    lengths = jnp.where(pick_row, SEQ_LEN // 10, lengths).astype(jnp.int32)
    borders = jnp.cumsum(lengths, axis=1).astype(jnp.int32)
    places = jnp.arange(SEQ_LEN, dtype=jnp.int32)
    document = jnp.sum((places[None, :, None] >= borders[:, None, :]).astype(jnp.int32), axis=2)
    starts = jnp.concatenate([jnp.zeros((SEQS, 1), jnp.int32), borders], axis=1)
    beginning = jnp.take_along_axis(starts, document, axis=1)
    return (document.reshape(TOKENS), (places[None, :] - beginning).reshape(TOKENS))


def draw_segments(key, part):
    return document_layout(key)[0]


def draw_positions(key, part):
    return document_layout(key)[1]


def draw_params(key, part):
    streams = jax.random.split(jax.random.fold_in(key, 5), 8)
    w_qkv = jax.random.normal(streams[0], (D, 3 * D), jnp.float32) / math.sqrt(D)
    w_dense = jax.random.normal(streams[1], (D, D), jnp.float32) / math.sqrt(32.0)
    w_up = jax.random.normal(streams[2], (D, FF), jnp.float32) / math.sqrt(D)
    w_down = jax.random.normal(streams[3], (FF, D), jnp.float32) / math.sqrt(FF)
    biases = 0.2 * jax.random.normal(streams[4], (4 * D + FF,), jnp.float32)
    gain_one = 1.0 + 0.1 * jax.random.normal(streams[5], (D,), jnp.float32)
    gain_two = 1.0 + 0.1 * jax.random.normal(streams[6], (D,), jnp.float32)
    shifts = 0.2 * jax.random.normal(streams[7], (2, D), jnp.float32)
    vector = jnp.concatenate([biases, gain_one, shifts[0], gain_two, shifts[1]])
    pieces = [w_qkv, w_dense, w_up, w_down, vector]
    row_block = jnp.concatenate([section.reshape(OWNERS, -1) for section in pieces], axis=1)
    return jnp.clip(row_block, -3.0, 3.0)


def steps_of(key, shape, cuts, least, largest):
    def one(dim, blocks):
        steps = jax.random.uniform(jax.random.fold_in(jax.random.fold_in(key, 6), dim), (blocks,), jnp.float32, least / len(cuts), largest / len(cuts))
        return jnp.repeat(jnp.exp(steps), shape[dim] // blocks).reshape((-1,) + (1,) * (len(shape) - dim - 1))

    factor_of = one(*cuts[0])
    for cut in cuts[1:]:
        factor_of = factor_of * one(*cut)
    return factor_of


def normal_values(key, shape, width, limit, cuts=(), kind=jnp.bfloat16):
    values = jax.random.normal(key, shape, jnp.float32) * width
    if len(cuts) > 0:
        values = steps_of(key, shape, cuts, -0.22, 0.18) * values
    return jnp.clip(values, min=-limit, max=limit).astype(kind)


def setup_inputs(seed: int = 0) -> dict:
    streams_of = jax.random.split(jax.random.key(seed), 8)
    return {
        "tokens": normal_values(streams_of[0], (TOKENS, D), 1.0, 6.0, ((0, 32),)),
        "out_grad": normal_values(streams_of[1], (TOKENS, D), 1.0, 6.0, ((0, 32),)),
        "segments": draw_segments(jax.random.fold_in(streams_of[7], 71), 0),
        "positions": draw_positions(jax.random.fold_in(streams_of[7], 71), 0),
        "params": draw_params(jax.random.fold_in(streams_of[7], 71), 0),
        "first_moment": normal_values(streams_of[5], (OWNERS, PARAM_DEV), (0.2 * NPARAM ** -0.5), 0.0009765625, ((0, 32),), jnp.float32),
        "second_moment": jnp.clip(jnp.exp(math.log(2.963128586941366e-08) - 2.089011 * jax.random.uniform(streams_of[6], (OWNERS, PARAM_DEV), jnp.float32) ** steps_of(streams_of[6], (OWNERS, PARAM_DEV), ((0, 32),), -0.2, 0.2)), 3.6686353954706874e-09, 2.963128586941366e-08),
    }


norm_eps = 1e-05
beta_first = 0.9
beta_second = 0.95
learn_rate = 0.01
weight_decay = 0.01
adam_eps = 1e-08
adam_steps = 3
rope_base = 10000.0

def split_rows(row_block, owners):
    height_list = [D, D, D, FF]
    breadth_list = [3 * D, D, FF, D]
    number = row_block.shape[0]
    pieces = []
    offset = 0
    for height, breadth in zip(height_list, breadth_list):
        extent = height // owners * breadth
        pieces.append(row_block[:, offset:offset + extent].reshape(number * (height // owners), breadth))
        offset += extent
    extent = (8 * D + FF) // owners
    pieces.append(row_block[:, offset:offset + extent].reshape(number * extent))
    return pieces

def pack_rows(pieces, owners):
    number = pieces[0].shape[0] // (D // owners)
    return jnp.concatenate([section.reshape(number, -1) for section in pieces], axis=1)

def split_vector(vector):
    lengths = [D, D, D, FF, D, D, D, D, D]
    pieces = []
    offset = 0
    for extent in lengths:
        pieces.append(vector[offset:offset + extent].astype(jnp.float32))
        offset += extent
    return pieces

def normalize(inputs):
    centred = inputs - lax.optimization_barrier(jnp.mean(inputs, axis=1, keepdims=True))
    inverse = lax.rsqrt(lax.optimization_barrier(jnp.mean(centred * centred, axis=1, keepdims=True)) + norm_eps)
    return (centred * inverse, inverse)

def rotary_tables(positions):
    halfway = ROT // 2
    frequency = jnp.power(rope_base, -jnp.arange(halfway, dtype=jnp.float32) * (2.0 / ROT))
    angles = positions.astype(jnp.float32)[:, None] * frequency[None, :]
    cosine = jnp.cos(angles)
    sine_table = jnp.sin(angles)
    return (jnp.concatenate([cosine, cosine], axis=1)[:, None, :], jnp.concatenate([sine_table, sine_table], axis=1)[:, None, :])

def rotate(tensor, cosine, sine_table):
    halfway = ROT // 2
    turned = tensor[..., :ROT]
    swapped = jnp.concatenate([-turned[..., halfway:], turned[..., :halfway]], axis=-1)
    return jnp.concatenate([turned * cosine + swapped * sine_table, tensor[..., ROT:]], axis=-1)

def rotate_back(tensor, cosine, sine_table):
    halfway = ROT // 2
    turned = tensor[..., :ROT]
    scaled = turned * sine_table
    swapped = jnp.concatenate([scaled[..., halfway:], -scaled[..., :halfway]], axis=-1)
    return jnp.concatenate([turned * cosine + swapped, tensor[..., ROT:]], axis=-1)

def gelu_exact(inputs):
    return 0.5 * inputs * (1.0 + lax.erf(inputs * 0.7071067811865476))

def gelu_slope(inputs):
    return 0.5 * (1.0 + lax.erf(inputs * 0.7071067811865476)) + inputs * jnp.exp(-0.5 * inputs * inputs) * 0.3989422804014327

def head_scores(query_rows, key_rows, allowed):
    scores = jnp.dot(query_rows, key_rows.T, preferred_element_type=jnp.float32) * HEAD_DIM ** (-0.5)
    return jnp.where(allowed, scores, -jnp.inf)

def head_forward(query_rows, key_rows, value_rows, allowed):
    scores = head_scores(query_rows, key_rows, allowed)
    highest = lax.optimization_barrier(jnp.max(scores, axis=1, keepdims=True))
    logsum = highest + jnp.log(lax.optimization_barrier(jnp.sum(jnp.exp(scores - highest), axis=1, keepdims=True)))
    weights = jnp.exp(scores - logsum).astype(jnp.bfloat16)
    output = jnp.dot(weights, value_rows, preferred_element_type=jnp.float32).astype(jnp.bfloat16)
    return (output, logsum[:, 0])

def head_backward(query_rows, key_rows, value_rows, output, grad_output, logsum, allowed):
    scores = head_scores(query_rows, key_rows, allowed)
    probability = jnp.exp(scores - logsum[:, None])
    grad_probability = jnp.dot(grad_output, value_rows.T, preferred_element_type=jnp.float32)
    row_delta = lax.optimization_barrier(jnp.sum(grad_output.astype(jnp.float32) * output.astype(jnp.float32), axis=1, keepdims=True))
    grad_scores = (probability * (grad_probability - row_delta) * HEAD_DIM ** (-0.5)).astype(jnp.bfloat16)
    grad_query = jnp.dot(grad_scores, key_rows, preferred_element_type=jnp.float32)
    grad_keys = jnp.dot(grad_scores.T, query_rows, preferred_element_type=jnp.float32)
    grad_values = jnp.dot(probability.astype(jnp.bfloat16).T, grad_output, preferred_element_type=jnp.float32)
    return (grad_query, grad_keys, grad_values)

def adam_update(params, grads, first_moment, second_moment, squares_total):
    clip_factor = jnp.minimum(1.0, 1.0 / jnp.sqrt(squares_total + 1e-12))
    clipped = grads * clip_factor
    new_first = beta_first * first_moment + (1.0 - beta_first) * clipped
    new_second = beta_second * second_moment + (1.0 - beta_second) * clipped * clipped
    corrected_first = new_first / (1.0 - beta_first ** adam_steps)
    corrected_second = new_second / (1.0 - beta_second ** adam_steps)
    new_params = params - learn_rate * (corrected_first / (jnp.sqrt(corrected_second) + adam_eps) + weight_decay * params)
    return (new_params, new_first, new_second)

def layer_pass(tokens, out_grad, segments, positions, weights):
    w_qkv, w_dense, w_up, w_down, vector = weights
    bias_q, bias_v, bias_dense, bias_up, bias_down, gain_one, shift_one, gain_two, shift_two = split_vector(vector)
    rows_here = tokens.shape[0]
    inputs = tokens.astype(jnp.float32)
    normed, inverse = normalize(inputs)
    attn_in = (normed * gain_one + shift_one).astype(jnp.bfloat16)
    mlp_in = (normed * gain_two + shift_two).astype(jnp.bfloat16)
    projected = jnp.dot(attn_in, w_qkv, preferred_element_type=jnp.float32)
    cosine, sine_table = rotary_tables(positions)
    query_all = rotate((projected[:, :D] + bias_q).reshape(rows_here, HEADS, HEAD_DIM), cosine, sine_table).astype(jnp.bfloat16)
    key_all = rotate(projected[:, D:2 * D].reshape(rows_here, HEADS, HEAD_DIM), cosine, sine_table).astype(jnp.bfloat16)
    value_all = (projected[:, 2 * D:] + bias_v).astype(jnp.bfloat16).reshape(rows_here, HEADS, HEAD_DIM)
    query_heads = query_all.transpose(1, 0, 2)
    key_heads = key_all.transpose(1, 0, 2)
    value_heads = value_all.transpose(1, 0, 2)
    places = jnp.arange(rows_here, dtype=jnp.int32)
    allowed = (places[None, :] <= places[:, None]) & (segments[None, :] == segments[:, None])

    def forward_head(bundle):
        return head_forward(bundle[0], bundle[1], bundle[2], allowed)
    outputs, logsums = lax.map(forward_head, (query_heads, key_heads, value_heads))
    attended = outputs.transpose(1, 0, 2).reshape(rows_here, D)
    attn_out = jnp.dot(attended, w_dense, preferred_element_type=jnp.float32) + bias_dense
    hidden_pre = jnp.dot(mlp_in, w_up, preferred_element_type=jnp.float32) + bias_up
    activated = gelu_exact(hidden_pre).astype(jnp.bfloat16)
    mlp_out = jnp.dot(activated, w_down, preferred_element_type=jnp.float32) + bias_down
    result = (inputs + attn_out + mlp_out).astype(jnp.bfloat16)
    cotangent = out_grad.astype(jnp.float32)
    grad_down = jnp.dot(activated.T, out_grad, preferred_element_type=jnp.float32)
    grad_bias_out = lax.optimization_barrier(jnp.sum(cotangent, axis=0))
    grad_hidden = jnp.dot(out_grad, w_down.T, preferred_element_type=jnp.float32) * gelu_slope(hidden_pre)
    grad_hidden_low = grad_hidden.astype(jnp.bfloat16)
    grad_up = jnp.dot(mlp_in.T, grad_hidden_low, preferred_element_type=jnp.float32)
    grad_bias_up = lax.optimization_barrier(jnp.sum(grad_hidden, axis=0))
    grad_mlp_in = jnp.dot(grad_hidden_low, w_up.T, preferred_element_type=jnp.float32)
    grad_dense = jnp.dot(attended.T, out_grad, preferred_element_type=jnp.float32)
    grad_attended = jnp.dot(out_grad, w_dense.T, preferred_element_type=jnp.float32).astype(jnp.bfloat16)
    grad_att_heads = grad_attended.reshape(rows_here, HEADS, HEAD_DIM).transpose(1, 0, 2)

    def backward_head(bundle):
        return head_backward(bundle[0], bundle[1], bundle[2], bundle[3], bundle[4], bundle[5], allowed)
    grad_qh, grad_kh, grad_vh = lax.map(backward_head, (query_heads, key_heads, value_heads, outputs, grad_att_heads, logsums))
    grad_query = rotate_back(grad_qh.transpose(1, 0, 2), cosine, sine_table).reshape(rows_here, D)
    grad_key = rotate_back(grad_kh.transpose(1, 0, 2), cosine, sine_table).reshape(rows_here, D)
    grad_value = grad_vh.transpose(1, 0, 2).reshape(rows_here, D)
    grad_low = jnp.concatenate([grad_query, grad_key, grad_value], axis=1).astype(jnp.bfloat16)
    grad_qkv = jnp.dot(attn_in.T, grad_low, preferred_element_type=jnp.float32)
    grad_attn_in = jnp.dot(grad_low, w_qkv.T, preferred_element_type=jnp.float32)
    grad_normed = grad_attn_in * gain_one + grad_mlp_in * gain_two
    grad_inputs = cotangent + inverse * (grad_normed - lax.optimization_barrier(jnp.mean(grad_normed, axis=1, keepdims=True)) - normed * lax.optimization_barrier(jnp.mean(grad_normed * normed, axis=1, keepdims=True)))
    grad_vector = jnp.concatenate([lax.optimization_barrier(jnp.sum(grad_query, axis=0)), lax.optimization_barrier(jnp.sum(grad_value, axis=0)), grad_bias_out, grad_bias_up, grad_bias_out, lax.optimization_barrier(jnp.sum(grad_attn_in * normed, axis=0)), lax.optimization_barrier(jnp.sum(grad_attn_in, axis=0)), lax.optimization_barrier(jnp.sum(grad_mlp_in * normed, axis=0)), lax.optimization_barrier(jnp.sum(grad_mlp_in, axis=0))])
    return (result, grad_inputs, (grad_qkv, grad_dense, grad_up, grad_down, grad_vector))

def reference(tokens, out_grad, segments, positions, params, first_moment, second_moment):
    weights = split_rows(params.astype(jnp.bfloat16), OWNERS)

    def one_sequence(totals, sequence):
        result, grad_inputs, grad_parts = layer_pass(sequence[0], sequence[1], sequence[2], sequence[3], weights)
        return (tuple((total + part_grad for total, part_grad in zip(totals, grad_parts))), (result, grad_inputs))
    empty_sums = tuple((jnp.zeros(section.shape, jnp.float32) for section in weights))
    inputs_seq = (tokens.reshape(SEQS, SEQ_LEN, D), out_grad.reshape(SEQS, SEQ_LEN, D), segments.reshape(SEQS, SEQ_LEN), positions.reshape(SEQS, SEQ_LEN))
    totals, (results, grad_inputs) = lax.scan(one_sequence, empty_sums, inputs_seq)
    grads = pack_rows(list(totals), OWNERS)
    squares_total = jnp.sum(grads * grads)
    new_params, new_first, new_second = adam_update(params, grads, first_moment, second_moment, squares_total)
    return (results.reshape(TOKENS, D), grad_inputs.reshape(TOKENS, D), grads, new_params, new_first, new_second)
```

```python
import functools

import jax
import jax.numpy as jnp
from jax import lax
from jax.experimental import pallas as pl
from jax.experimental.pallas import tpu as pltpu
from jax.sharding import PartitionSpec as P

D = 768
HEADS = 12
HEAD_DIM = 64
ROT = 16
FF = 3072
HALF = D // 2
FFH = FF // 2
NVEC = 8 * D + FF
AX = ("dp", "ctx")
BF = jnp.bfloat16
F32 = jnp.float32

norm_eps = 1e-05
beta_first = 0.9
beta_second = 0.95
learn_rate = 0.01
weight_decay = 0.01
adam_eps = 1e-08
adam_steps = 3
rope_base = 10000.0
NEG = -1e30


def swap(value, mask):
    size = lax.axis_size("dp") * lax.axis_size("ctx")
    return lax.ppermute(value, AX, [(i, i ^ mask) for i in range(size)])


def pick(value, index, axis):
    return lax.dynamic_index_in_dim(value, index, axis, keepdims=False)


def gather_pair(both, rows_a):
    z_all = jnp.stack([both, swap(both, 8), swap(both, 16), swap(both, 24)])
    part_a, part_b = z_all[:, :rows_a], z_all[:, rows_a:]
    eight_a = jnp.stack([part_a, swap(part_a, 1)])
    eight_b = jnp.stack([part_b, swap(part_b, 4)])
    return eight_a, swap(eight_a, 4), eight_b, swap(eight_b, 1)


def rel_places(me, rel_z, rel_y, rel_x):
    outer = lax.shift_right_logical(me, 2)
    return outer ^ (rel_z * 2 + rel_y), (me & 1) ^ rel_x


def copy_all(copies):
    for one in copies:
        one.start()
    for one in copies:
        one.wait()


def assemble_pair_kernel(me_ref, a8, ay, b8, bx, out, sems):
    me = me_ref[0]
    copies = []
    for j in range(16):
        rel_z, rel_y, rel_x = j >> 2, (j >> 1) & 1, j & 1
        outer, xx = rel_places(me, rel_z, rel_y, rel_x)
        src_a = (ay if rel_y else a8).at[rel_x, rel_z]
        src_b = (bx if rel_x else b8).at[rel_y, rel_z]
        copies.append(pltpu.make_async_copy(src_a, out.at[outer, 0, xx], sems.at[2 * j]))
        copies.append(pltpu.make_async_copy(src_b, out.at[outer, 1, xx], sems.at[2 * j + 1]))
    copy_all(copies)


def assemble_down_kernel(me_ref, a8, ay, b8, bx, down, dense, sems):
    me = me_ref[0]
    copies = []
    for j in range(16):
        rel_z, rel_y, rel_x = j >> 2, (j >> 1) & 1, j & 1
        outer, xx = rel_places(me, rel_z, rel_y, rel_x)
        src_a = (ay if rel_y else a8).at[rel_x, rel_z]
        src_b = (bx if rel_x else b8).at[rel_y, rel_z]
        copies.append(pltpu.make_async_copy(src_a, down.at[outer, xx, pl.ds(0, 64)], sems.at[j]))
        copies.append(
            pltpu.make_async_copy(
                src_b.at[pl.ds(0, 32)], down.at[outer, xx, pl.ds(64, 32)], sems.at[16 + j]
            )
        )
        copies.append(
            pltpu.make_async_copy(src_b.at[pl.ds(32, 24)], dense.at[outer, xx], sems.at[32 + j])
        )
    copy_all(copies)


def whole(shape):
    return pl.BlockSpec(shape, lambda *_: (0,) * len(shape))


def assemble(kernel, me, pieces, shapes, sem_count):
    return pl.pallas_call(
        kernel,
        out_shape=[jax.ShapeDtypeStruct(s, BF) for s in shapes],
        in_specs=[pl.BlockSpec(memory_space=pltpu.SMEM)]
        + [pl.BlockSpec(memory_space=pl.ANY)] * 4,
        out_specs=[pl.BlockSpec(memory_space=pltpu.VMEM) for _ in shapes],
        scratch_shapes=[pltpu.SemaphoreType.DMA((sem_count,))],
        cost_estimate=pl.CostEstimate(flops=0, bytes_accessed=5_000_000, transcendentals=0),
    )(me.reshape(1), *pieces)


def rope_chunk(u, cosine, low, high):
    return u * cosine + pltpu.roll(u, 120, 1) * low + pltpu.roll(u, 8, 1) * high


def norm_rows(x_ref):
    inputs = x_ref[...].astype(F32)
    centred = inputs - jnp.mean(inputs, axis=1, keepdims=True)
    inverse = lax.rsqrt(jnp.mean(centred * centred, axis=1, keepdims=True) + norm_eps)
    return centred * inverse, inverse


def qkv_kernel(x_ref, w_ref, vec_ref, bias_ref, c_ref, lo_ref, hi_ref, q_ref, k_ref, v_ref, a1_ref, a2_ref):
    normed, _ = norm_rows(x_ref)
    a1 = (normed * vec_ref[0:1, :] + vec_ref[1:2, :]).astype(BF)
    a1_ref[...] = a1
    a2_ref[...] = (normed * vec_ref[2:3, :] + vec_ref[3:4, :]).astype(BF)
    proj = jnp.dot(a1, w_ref[:, : 3 * HALF], preferred_element_type=F32)
    cosine, low, high = c_ref[...], lo_ref[...], hi_ref[...]
    for j in range(3):
        at = slice(128 * j, 128 * j + 128)
        q = proj[:, 128 * j : 128 * j + 128] + bias_ref[0:1, at]
        q_ref[:, at] = (rope_chunk(q, cosine, low, high).astype(BF).astype(F32) * 0.125).astype(BF)
        k = proj[:, HALF + 128 * j : HALF + 128 * j + 128]
        k_ref[:, at] = rope_chunk(k, cosine, low, high).astype(BF)
    v_ref[...] = (proj[:, 2 * HALF :] + bias_ref[1:2, :]).astype(BF)


def far_kernel(used_ref, x_ref, w_ref, vec_ref, bias_ref, c_ref, lo_ref, hi_ref, k_ref, v_ref, a1_ref):
    @pl.when(used_ref[0] > 0)
    def _():
        normed, _ = norm_rows(x_ref)
        a1 = (normed * vec_ref[0:1, :] + vec_ref[1:2, :]).astype(BF)
        a1_ref[...] = a1
        proj = jnp.dot(a1, w_ref[:, HALF : 3 * HALF], preferred_element_type=F32)
        cosine, low, high = c_ref[...], lo_ref[...], hi_ref[...]
        for j in range(3):
            at = slice(128 * j, 128 * j + 128)
            k = proj[:, 128 * j : 128 * j + 128]
            k_ref[:, at] = rope_chunk(k, cosine, low, high).astype(BF)
        v_ref[...] = (proj[:, HALF:] + bias_ref[1:2, :]).astype(BF)

    @pl.when(used_ref[0] == 0)
    def _():
        k_ref[...] = jnp.zeros_like(k_ref)
        v_ref[...] = jnp.zeros_like(v_ref)
        a1_ref[...] = jnp.zeros_like(a1_ref)


def run_qkv(x, w, vecs, biases, tables, used=None):
    rows = x.shape[0]
    blk = 256
    row = lambda cols: pl.BlockSpec((blk, cols), lambda i, *_: (i, 0))
    specs = [row(D), whole(w.shape), whole(vecs.shape), whole(biases.shape)] + [row(128)] * 3
    wide = lambda cols: jax.ShapeDtypeStruct((rows, cols), BF)
    cost = pl.CostEstimate(flops=2 * rows * D * 3 * HALF, bytes_accessed=8_000_000, transcendentals=0)
    if used is None:
        return pl.pallas_call(
            qkv_kernel,
            grid=(rows // blk,),
            in_specs=specs,
            out_specs=[row(HALF)] * 3 + [row(D)] * 2,
            out_shape=[wide(HALF)] * 3 + [wide(D)] * 2,
            cost_estimate=cost,
        )(x, w, vecs, biases, *tables)
    return pl.pallas_call(
        far_kernel,
        grid_spec=pltpu.PrefetchScalarGridSpec(
            num_scalar_prefetch=1,
            grid=(rows // blk,),
            in_specs=specs,
            out_specs=[row(HALF)] * 2 + [row(D)],
        ),
        out_shape=[wide(HALF)] * 2 + [wide(D)],
        cost_estimate=cost,
    )(used, x, w, vecs, biases, *tables)


QB = 256


def variants(rows):
    cases = []
    for qb in range(rows // QB):
        for near in range(qb + 1):
            if near == 0:
                cases += [(qb, 0, far) for far in range(rows // QB + 1)]
            else:
                cases.append((qb, near, 0))
    return cases


def load_keys(far_ref, near_ref, rows, qb, near, far):
    parts = []
    if far:
        parts.append(far_ref[rows - far * QB : rows, :])
    parts.append(near_ref[near * QB : (qb + 1) * QB, :])
    return parts[0] if len(parts) == 1 else jnp.concatenate(parts, axis=0)


def attn_fwd_kernel(rows, plan_ref, q_ref, k_ref, v_ref, kf_ref, vf_ref, start_ref, o_ref, lse_ref):
    seq = pl.program_id(0)
    lane = lax.broadcasted_iota(jnp.int32, (QB, 128), 1)
    blocks = rows // QB
    for qb, near, far in variants(rows):
        low = plan_ref[seq * blocks + qb]
        match = low == (near if far == 0 else -far)

        @pl.when(match)
        def _(qb=qb, near=near, far=far):
            keys = load_keys(kf_ref, k_ref, rows, qb, near, far)
            values = load_keys(vf_ref, v_ref, rows, qb, near, far)
            count = keys.shape[0]
            first = near * QB - far * QB
            q = q_ref[qb * QB : (qb + 1) * QB, :]
            start = start_ref[qb * QB : (qb + 1) * QB, :]
            key_at = lax.broadcasted_iota(jnp.int32, (QB, count), 1) + first
            query_at = lax.broadcasted_iota(jnp.int32, (QB, count), 0) + qb * QB
            ok = (key_at >= start) & (key_at <= query_at)
            outs, lses = [], []
            for head in range(2):
                mine = (lane < 64) if head == 0 else (lane >= 64)
                qh = jnp.where(mine, q, jnp.zeros_like(q))
                s = lax.dot_general(qh, keys, (((1,), (1,)), ((), ())), preferred_element_type=F32)
                s = jnp.where(ok, s, NEG)
                top = jnp.max(s, axis=1, keepdims=True)
                e = jnp.exp(s - top)
                total = jnp.sum(e, axis=1, keepdims=True)
                prob = (e * (1.0 / total)).astype(BF)
                outs.append(jnp.dot(prob, values, preferred_element_type=F32))
                lses.append(jnp.broadcast_to(top + jnp.log(total), (QB, 128)))
            o_ref[qb * QB : (qb + 1) * QB, :] = jnp.where(lane < 64, outs[0], outs[1]).astype(BF)
            lse_ref[qb * QB : (qb + 1) * QB, :] = jnp.where(lane < 64, lses[0], lses[1])


def attn_bwd_kernel(
    rows, plan_ref, q_ref, k_ref, v_ref, kf_ref, vf_ref, start_ref, o_ref, do_ref, lse_ref,
    c_ref, lo_ref, hi_ref, cf_ref, lof_ref, hif_ref,
    dq_ref, dk_ref, dv_ref, dkf_ref, dvf_ref, sum_ref, dk_acc, dv_acc, lse_t, delta_t, start_t,
):
    seq = pl.program_id(0)
    blocks = rows // QB
    lane = lax.broadcasted_iota(jnp.int32, (QB, 128), 1)
    sub = lax.broadcasted_iota(jnp.int32, (128, QB), 0)
    dk_acc[...] = jnp.zeros_like(dk_acc)
    dv_acc[...] = jnp.zeros_like(dv_acc)
    lse_t[...] = jnp.transpose(lse_ref[...])
    delta_t[...] = jnp.transpose(do_ref[...].astype(F32) * o_ref[...].astype(F32))
    start_t[...] = jnp.transpose(jnp.broadcast_to(start_ref[...], (rows, 128)).astype(F32))[0:8, :]
    for qb, near, far in variants(rows):
        low = plan_ref[seq * blocks + qb]
        match = low == (near if far == 0 else -far)

        @pl.when(match)
        def _(qb=qb, near=near, far=far):
            keys = load_keys(kf_ref, k_ref, rows, qb, near, far)
            values = load_keys(vf_ref, v_ref, rows, qb, near, far)
            count = keys.shape[0]
            first = near * QB - far * QB
            at = slice(qb * QB, (qb + 1) * QB)
            q, do = q_ref[at, :], do_ref[at, :]
            start = start_t[0:1, at]
            key_at = lax.broadcasted_iota(jnp.int32, (count, QB), 0) + first
            query_at = lax.broadcasted_iota(jnp.int32, (count, QB), 1) + qb * QB
            ok = (key_at >= start.astype(jnp.int32)) & (key_at <= query_at)
            keys_t = jnp.transpose(keys)
            dqs, dk, dv = [], None, None
            for head in range(2):
                mine = (lane < 64) if head == 0 else (lane >= 64)
                hs = slice(64 * head, 64 * head + 64)
                qh = jnp.where(mine, q, jnp.zeros_like(q))
                doh = jnp.where(mine, do, jnp.zeros_like(do))
                lse = lse_t[64 * head : 64 * head + 1, at]
                delta = jnp.sum(delta_t[hs, at], axis=0, keepdims=True)
                nt = (((1,), (1,)), ((), ()))
                s = lax.dot_general(keys, qh, nt, preferred_element_type=F32)
                prob = jnp.where(ok, jnp.exp(s - lse), 0.0)
                dprob = lax.dot_general(values, doh, nt, preferred_element_type=F32)
                ds = (prob * (dprob - delta)).astype(BF)
                dv_h = jnp.dot(prob.astype(BF), doh, preferred_element_type=F32)
                dk_h = jnp.dot(ds, qh, preferred_element_type=F32)
                dv = dv_h if dv is None else dv + dv_h
                dk = dk_h if dk is None else dk + dk_h
                dqs.append(jnp.dot(keys_t, ds, preferred_element_type=F32))
            dq = jnp.transpose(jnp.where(sub < 64, dqs[0], dqs[1])) * 0.125
            dq = rope_chunk(dq, c_ref[at, :], -lo_ref[at, :], -hi_ref[at, :])
            dq_ref[at, :] = dq.astype(BF)
            part = jnp.sum(dq, axis=0, keepdims=True)
            if qb == 0:
                sum_ref[0:1, :] = part
            else:
                sum_ref[0:1, :] += part
            span = slice(rows + first, rows + first + count)
            dk_acc[span, :] += dk
            dv_acc[span, :] += dv
    dk_ref[...] = rope_chunk(dk_acc[rows:, :], c_ref[...], -lo_ref[...], -hi_ref[...]).astype(BF)
    dkf_ref[...] = rope_chunk(dk_acc[:rows, :], cf_ref[...], -lof_ref[...], -hif_ref[...]).astype(BF)
    dv_ref[...] = dv_acc[rows:, :].astype(BF)
    dvf_ref[...] = dv_acc[:rows, :].astype(BF)
    sum_ref[1:2, :] = jnp.sum(dv_acc[...], axis=0, keepdims=True)
    sum_ref[2:8, :] = jnp.zeros((6, 128), F32)


def attn_specs(rows):
    block = pl.BlockSpec((rows, 128), lambda s, p, *_: (s, p))
    per_seq = lambda cols: pl.BlockSpec((rows, cols), lambda s, p, *_: (s, 0))
    return block, per_seq


def attn_fwd(plan, q, k, v, kf, vf, start):
    total = q.shape[0]
    rows = total // 2
    block, per_seq = attn_specs(rows)
    return pl.pallas_call(
        functools.partial(attn_fwd_kernel, rows),
        grid_spec=pltpu.PrefetchScalarGridSpec(
            num_scalar_prefetch=1,
            grid=(2, HALF // 128),
            in_specs=[block] * 5 + [per_seq(1)],
            out_specs=[block] * 2,
        ),
        out_shape=[
            jax.ShapeDtypeStruct((total, HALF), BF),
            jax.ShapeDtypeStruct((total, HALF), F32),
        ],
        cost_estimate=pl.CostEstimate(
            flops=20_000_000_000, bytes_accessed=6_000_000, transcendentals=0
        ),
    )(plan, q, k, v, kf, vf, start)


def attn_bwd(plan, q, k, v, kf, vf, start, o, do, lse, tables, tables_far):
    total = q.shape[0]
    rows = total // 2
    block, per_seq = attn_specs(rows)
    wide = jax.ShapeDtypeStruct((total, HALF), BF)
    return pl.pallas_call(
        functools.partial(attn_bwd_kernel, rows),
        grid_spec=pltpu.PrefetchScalarGridSpec(
            num_scalar_prefetch=1,
            grid=(2, HALF // 128),
            in_specs=[block] * 5 + [per_seq(1)] + [block] * 3 + [per_seq(128)] * 6,
            out_specs=[block] * 5 + [pl.BlockSpec((8, 128), lambda s, p, *_: (s, p))],
            scratch_shapes=[pltpu.VMEM((2 * rows, 128), F32)] * 2
            + [pltpu.VMEM((128, rows), F32)] * 2
            + [pltpu.VMEM((8, rows), F32)],
        ),
        out_shape=[wide] * 5 + [jax.ShapeDtypeStruct((16, HALF), F32)],
        cost_estimate=pl.CostEstimate(
            flops=40_000_000_000, bytes_accessed=10_000_000, transcendentals=0
        ),
    )(plan, q, k, v, kf, vf, start, o, do, lse, *tables, *tables_far)


def rotary_tables(positions):
    halfway = ROT // 2
    frequency = jnp.power(rope_base, -jnp.arange(halfway, dtype=F32) * (2.0 / ROT))
    lane = jnp.arange(128) % HEAD_DIM
    angles = positions.astype(F32)[:, None] * frequency[lane % halfway][None, :]
    sine = jnp.sin(angles)
    cosine = jnp.where(lane < ROT, jnp.cos(angles), 1.0)
    low = jnp.where(lane < halfway, -sine, 0.0)
    high = jnp.where((lane >= halfway) & (lane < ROT), sine, 0.0)
    return cosine, low, high


def gelu_exact(inputs):
    return 0.5 * inputs * (1.0 + lax.erf(inputs * 0.7071067811865476))


def gelu_slope(inputs):
    return (
        0.5 * (1.0 + lax.erf(inputs * 0.7071067811865476))
        + inputs * jnp.exp(-0.5 * inputs * inputs) * 0.3989422804014327
    )


def normalize(inputs):
    centred = inputs - jnp.mean(inputs, axis=1, keepdims=True)
    inverse = lax.rsqrt(jnp.mean(centred * centred, axis=1, keepdims=True) + norm_eps)
    return (centred * inverse, inverse)


def adam_update(params, grads, first_moment, second_moment, squares_total):
    clip_factor = jnp.minimum(1.0, 1.0 / jnp.sqrt(squares_total + 1e-12))
    clipped = grads * clip_factor
    new_first = beta_first * first_moment + (1.0 - beta_first) * clipped
    new_second = beta_second * second_moment + (1.0 - beta_second) * clipped * clipped
    corrected_first = new_first / (1.0 - beta_first**adam_steps)
    corrected_second = new_second / (1.0 - beta_second**adam_steps)
    new_params = params - learn_rate * (
        corrected_first / (jnp.sqrt(corrected_second) + adam_eps) + weight_decay * params
    )
    return (new_params, new_first, new_second)


def split_shard(flat, owners):
    pieces, offset = [], 0
    for height, breadth in ((D, 3 * D), (D, D), (D, FF), (FF, D)):
        extent = height // owners * breadth
        pieces.append(flat[offset : offset + extent].reshape(height // owners, breadth))
        offset += extent
    pieces.append(flat[offset:])
    return pieces


def core_parts(qkv, dense):
    parts = []
    for c in range(2):
        cols = [qkv[:, D * j + HALF * c : D * j + HALF * c + HALF] for j in range(3)]
        parts.append((jnp.concatenate(cols, axis=1), dense[:, HALF * c : HALF * c + HALF]))
    return parts


def up_halves(up, group):
    rows = up.shape[0]
    four = up.reshape(rows, FF // (2 * group), 2, group)
    return four[:, :, 0].reshape(rows, FFH), four[:, :, 1].reshape(rows, FFH)


def gather_staged(me, core, qkv, dense, up, down, vector):
    group = 2 * down.shape[0]
    rows = qkv.shape[0]
    ups = up_halves(up, group)
    halves = core_parts(qkv, dense)
    lanes = jnp.pad(vector, (0, 384 - vector.shape[0])).reshape(3, 128)
    lanes = jnp.pad(lanes, ((0, rows - 3), (0, 0)))
    packed = [
        jnp.concatenate([halves[c][0], lanes, ups[c], halves[c][1]], axis=1) for c in range(2)
    ]
    is_zero = core == 0
    mine = jnp.where(is_zero, packed[0], packed[1])
    other = swap(jnp.where(is_zero, packed[1], packed[0]), 2)
    pair = jnp.where(is_zero, jnp.stack([mine, other]), jnp.stack([other, mine]))
    q_end, u_end = 3 * HALF + 128, 3 * HALF + 128 + FFH
    q_pieces = gather_pair(pair[:, :, :q_end], 1)
    u_pieces = gather_pair(pair[:, :, q_end:u_end], 1)
    dense_rows = jnp.concatenate([pair[0, :, u_end:], pair[1, :, u_end:]], axis=1)
    d_pieces = gather_pair(jnp.concatenate([down, dense_rows], axis=0), 64)
    return q_pieces, u_pieces, d_pieces


def finish_vector(w_q):
    lanes = w_q[:, :, :, :3, 3 * HALF :].reshape(32, 384)
    return lanes[:, : NVEC // 32].reshape(NVEC)


def split_vector(vector):
    pieces, offset = [], 0
    for extent in [D, D, D, FF, D, D, D, D, D]:
        pieces.append(vector[offset : offset + extent].astype(F32))
        offset += extent
    return pieces


def scatter_pair(part_a, part_b, place):
    z, y, x = place
    send_a = pick(part_a, 1 - x, 2).astype(BF)
    send_b = pick(part_b, 1 - y, 2).astype(BF)
    got_a, got_b = swap(send_a, 1), swap(send_b, 4)
    sum_a = pick(part_a, x, 2) + got_a.astype(F32)
    sum_b = pick(part_b, y, 2) + got_b.astype(F32)
    got_a = swap(pick(sum_a, 1 - y, 1).astype(BF), 4)
    got_b = swap(pick(sum_b, 1 - x, 1).astype(BF), 1)
    sum_a = pick(sum_a, y, 1) + got_a.astype(F32)
    sum_b = pick(sum_b, x, 1) + got_b.astype(F32)
    both = jnp.concatenate([sum_a, sum_b], axis=1)
    total = pick(both, z, 0)
    for k in (1, 2, 3):
        total = total + swap(pick(both, z ^ k, 0).astype(BF), 8 * k).astype(F32)
    return total


def on_device(tokens, out_grad, segments, positions, params, first_moment, second_moment):
    owners = lax.axis_size("dp") * lax.axis_size("ctx")
    staged = owners == 32
    me = (lax.axis_index("dp") * lax.axis_size("ctx") + lax.axis_index("ctx")).astype(jnp.int32)
    ctx, core = me & 1, (me >> 1) & 1
    is_zero = core == 0
    rows = tokens.shape[0]
    flat = params.reshape(-1)
    qkv, dense, up, down, vector = split_shard(flat.astype(BF), owners)
    group = 2 * down.shape[0]

    far_own = lax.ppermute(tokens, AX, [(i, i + 1) for i in range(0, owners, 2)])
    tokens_other = swap(tokens, 2)
    grad_other = swap(out_grad, 2)
    positions_all = jnp.concatenate([positions, swap(positions, 2)])

    if staged:
        q_pieces, u_pieces, d_pieces = gather_staged(me, core, qkv, dense, up, down, vector)
        w_q5 = assemble(assemble_pair_kernel, me, [p.reshape(p.shape[:2] + p.shape[-2:]) for p in q_pieces],
                        [(8, 2, 2, D // 32, 3 * HALF + 128)], 32)[0]
        w_u5 = assemble(assemble_pair_kernel, me, [p.reshape(p.shape[:2] + p.shape[-2:]) for p in u_pieces],
                        [(8, 2, 2, D // 32, FFH)], 32)[0]
        w_d4, dense5 = assemble(assemble_down_kernel, me, d_pieces,
                                [(8, 2, FF // 32, D), (8, 2, D // 32, D)], 48)
        vector = finish_vector(w_q5)
        w_q = w_q5.reshape(D, 3 * HALF + 128)
        w_up = w_u5.reshape(D, FFH)
        w_down = w_d4.reshape(FFH, D)
        dense_mine = dense5.reshape(8, 2, D // 32, 2, HALF).transpose(0, 3, 1, 2, 4).reshape(D, HALF)
        dense_got = swap(dense_mine, 2)
        w_dense = jnp.where(
            is_zero,
            jnp.concatenate([dense_mine, dense_got], axis=1),
            jnp.concatenate([dense_got, dense_mine], axis=1),
        )
    else:
        full = [lax.all_gather(p, AX, axis=0, tiled=True) for p in (qkv, dense, up, down, vector)]
        w_q = pick(full[0].reshape(D, 3, 2, HALF), core, 2).reshape(D, 3 * HALF)
        w_dense = full[1]
        w_up = pick(full[2].reshape(D, FFH // group, 2, group), core, 2).reshape(D, FFH)
        w_down = pick(full[3].reshape(FFH // group, 2, group, D), core, 1).reshape(FFH, D)
        vector = full[4]
    bias_q, bias_v, bias_dense, bias_up, bias_down, gain_one, shift_one, gain_two, shift_two = (
        split_vector(vector)
    )
    half_of = lambda v: jnp.where(is_zero, v[:HALF], v[HALF:])
    bias_up_half = pick(bias_up.reshape(FFH // group, 2, group), core, 1).reshape(FFH)
    dense_rows = lax.dynamic_slice_in_dim(w_dense, core * HALF, HALF, 0)
    vecs = jnp.stack([gain_one, shift_one, gain_two, shift_two] + [jnp.zeros_like(gain_one)] * 4)
    biases = jnp.stack([half_of(bias_q), half_of(bias_v)] + [jnp.zeros((HALF,), F32)] * 6)

    x_all = jnp.concatenate([tokens, tokens_other], axis=0)
    g_all = jnp.concatenate([out_grad, grad_other], axis=0)
    x_far = jnp.concatenate([far_own, swap(far_own, 2)], axis=0)
    local = jnp.arange(rows, dtype=jnp.int32)
    start = (jnp.concatenate([local, local]) - positions_all)[:, None]
    heads_pos = positions_all.reshape(2, rows)[:, :1]
    far_positions = jnp.maximum(heads_pos - rows + local[None, :], 0).reshape(-1)
    tables = rotary_tables(positions_all)
    tables_far = rotary_tables(far_positions)
    least = jnp.min(start.reshape(-1, QB), axis=1)
    blocks = rows // QB
    plan = jnp.where(least < 0, -((QB - 1 - least) // QB), least // QB)
    used = ctx.reshape(1)

    q, k, v, a1, a2 = run_qkv(x_all, w_q, vecs, biases, tables)
    kf, vf, a1f = run_qkv(x_far, w_q, vecs, biases, tables_far, used)
    att, lse = attn_fwd(plan, q, k, v, kf, vf, start)

    pre = jnp.dot(a2, w_up, preferred_element_type=F32) + bias_up_half
    act = gelu_exact(pre).astype(BF)
    grad_down = jnp.dot(act.T, g_all, preferred_element_type=F32)
    grad_dense = jnp.dot(att.T, g_all, preferred_element_type=F32)
    grad_pre = jnp.dot(g_all, w_down.T, preferred_element_type=F32) * gelu_slope(pre)
    grad_pre_low = grad_pre.astype(BF)
    grad_bias_up = jnp.sum(grad_pre, axis=0)
    grad_up = jnp.dot(a2.T, grad_pre_low, preferred_element_type=F32)

    grad_att = jnp.dot(g_all, dense_rows.T, preferred_element_type=F32).astype(BF)
    gq, gk, gv, gkf, gvf, sums = attn_bwd(
        plan, q, k, v, kf, vf, start, att, grad_att, lse, tables, tables_far
    )
    gkv = jnp.concatenate([gk, gv], axis=1)
    gkvf = jnp.concatenate([gkf, gvf], axis=1)
    grad_q_cols = jnp.dot(a1.T, gq, preferred_element_type=F32)
    grad_kv_cols = jnp.dot(a1.T, gkv, preferred_element_type=F32) + jnp.dot(
        a1f.T, gkvf, preferred_element_type=F32
    )
    grad_qkv = jnp.concatenate([grad_q_cols, grad_kv_cols], axis=1)

    normed, inverse = normalize(x_all.astype(F32))
    normed_far, _ = normalize(x_far.astype(F32))
    w_qkv = w_q[:, : 3 * HALF]
    ga1 = jnp.dot(gq, w_qkv[:, :HALF].T, preferred_element_type=F32) + jnp.dot(
        gkv, w_qkv[:, HALF:].T, preferred_element_type=F32
    )
    ga1f = jnp.dot(gkvf, w_qkv[:, HALF:].T, preferred_element_type=F32)
    ga2 = jnp.dot(grad_pre_low, w_up.T, preferred_element_type=F32)
    grad_gain_one = jnp.sum(ga1 * normed, axis=0) + jnp.sum(ga1f * normed_far, axis=0)
    grad_shift_one = jnp.sum(ga1, axis=0) + jnp.sum(ga1f, axis=0)
    grad_gain_two = jnp.sum(ga2 * normed, axis=0)
    grad_shift_two = jnp.sum(ga2, axis=0)

    cotangent = out_grad.astype(F32)
    grad_bias_out = jnp.sum(cotangent, axis=0)
    sums = jnp.sum(sums.reshape(2, 8, HALF), axis=0)
    nothing = jnp.zeros((HALF,), F32)
    spread = lambda v: jnp.where(
        is_zero, jnp.concatenate([v, nothing]), jnp.concatenate([nothing, v])
    )
    up_groups = grad_bias_up.reshape(FFH // group, group)
    up_zero = jnp.zeros_like(up_groups)
    grad_bias_up_full = jnp.where(
        is_zero,
        jnp.stack([up_groups, up_zero], axis=1),
        jnp.stack([up_zero, up_groups], axis=1),
    ).reshape(FF)
    grad_vector = jnp.concatenate(
        [
            spread(sums[0]),
            spread(sums[1]),
            grad_bias_out,
            grad_bias_up_full,
            grad_bias_out,
            grad_gain_one,
            grad_shift_one,
            grad_gain_two,
            grad_shift_two,
        ]
    )

    if staged:
        per = D // 32
        z, y, x = me >> 3, (me >> 2) & 1, ctx
        place = (z, y, x)
        dense_cols = [grad_dense[:, :HALF], grad_dense[:, HALF:]]
        keep = jnp.where(is_zero, dense_cols[0], dense_cols[1])
        got = swap(jnp.where(is_zero, dense_cols[1], dense_cols[0]), 2)
        dense_half = jnp.where(
            is_zero,
            jnp.concatenate([keep, got], axis=0),
            jnp.concatenate([got, keep], axis=0),
        )
        d6 = dense_half.reshape(4, 2, 2, 2, per, HALF)
        dn = grad_down.reshape(4, 2, 2, FF // 32, D)
        dense_wide = jnp.concatenate([d6[:, :, 0], d6[:, :, 1]], axis=-1)
        part_b = jnp.concatenate([dn[:, :, :, 64:], dense_wide], axis=3)
        done_d = scatter_pair(dn[:, :, :, :64], part_b.transpose(0, 2, 1, 3, 4), place)
        up6 = grad_up.reshape(4, 2, 2, 2, per, FFH)
        done_u = scatter_pair(up6[:, :, 0], up6[:, :, 1].transpose(0, 2, 1, 3, 4), place)
        lanes = jnp.pad(grad_vector.reshape(32, NVEC // 32), ((0, 0), (0, 384 - NVEC // 32)))
        lanes = jnp.pad(lanes.reshape(32, 3, 128), ((0, 0), (0, per - 3), (0, 0)))
        grad_q = jnp.concatenate([grad_qkv, lanes.reshape(D, 128)], axis=1)
        q6 = grad_q.reshape(4, 2, 2, 2, per, 3 * HALF + 128)
        done_q = scatter_pair(q6[:, :, 0], q6[:, :, 1].transpose(0, 2, 1, 3, 4), place)

        def core_swap(first, second):
            kept = jnp.where(is_zero, first, second)
            return kept, swap(jnp.where(is_zero, second, first), 2)

        def in_order(kept, got, axis):
            return jnp.where(
                is_zero,
                jnp.concatenate([kept, got], axis=axis),
                jnp.concatenate([got, kept], axis=axis),
            )

        q_keep, q_got = core_swap(done_q[:per], done_q[per:])
        u_keep, u_got = core_swap(done_u[:per], done_u[per:])
        e_keep, e_got = core_swap(
            done_d[FF // 32 :, :HALF], done_d[FF // 32 :, HALF:]
        )
        own_qkv = jnp.concatenate(
            [
                in_order(q_keep[:, HALF * j : HALF * j + HALF], q_got[:, HALF * j : HALF * j + HALF], 1)
                for j in range(3)
            ],
            axis=1,
        )
        own_vec = (q_keep[:3, 3 * HALF :] + q_got[:3, 3 * HALF :]).reshape(384)[: NVEC // 32]
        own_dense = in_order(e_keep, e_got, 1)
        three = lambda t: t.reshape(per, FFH // group, 1, group)
        own_up = in_order(three(u_keep), three(u_got), 2).reshape(per, FF)
        own_down = done_d[: FF // 32]
    else:
        widen = lambda t, axis: lax.dynamic_update_slice_in_dim(
            jnp.zeros(t.shape[:axis] + (2,) + t.shape[axis + 1 :], F32), t, core, axis
        )
        scatter = lambda t: lax.psum_scatter(t, AX, scatter_dimension=0, tiled=True)
        own_qkv = scatter(widen(grad_qkv.reshape(D, 3, 1, HALF), 2).reshape(D, 3 * D))
        own_dense = scatter(widen(grad_dense.reshape(1, HALF, D), 0).reshape(D, D))
        own_up = scatter(widen(grad_up.reshape(D, FFH // group, 1, group), 2).reshape(D, FF))
        own_down = scatter(widen(grad_down.reshape(FFH // group, 1, group, D), 1).reshape(FF, D))
        own_vec = scatter(grad_vector)

    grads = jnp.concatenate(
        [own_qkv.reshape(-1), own_dense.reshape(-1), own_up.reshape(-1), own_down.reshape(-1), own_vec]
    )
    squares = jnp.broadcast_to(jnp.sum(grads * grads), (8, 128))
    bit = 1
    while bit < owners:
        squares = squares + swap(squares, bit)
        bit *= 2
    new_params, new_first, new_second = adam_update(
        flat, grads, first_moment.reshape(-1), second_moment.reshape(-1), squares[0, 0]
    )

    partial_result = jnp.dot(att, dense_rows, preferred_element_type=F32) + jnp.dot(
        act, w_down, preferred_element_type=F32
    )
    result = (
        tokens.astype(F32)
        + partial_result[:rows]
        + swap(partial_result[rows:], 2)
        + (bias_dense + bias_down)
    ).astype(BF)
    gx = ga1 * gain_one + ga2 * gain_two
    gx_far = ga1f * gain_one
    far_total = gx_far[:rows] + swap(gx_far[rows:], 2)
    from_later = lax.ppermute(far_total.astype(BF), AX, [(i + 1, i) for i in range(0, owners, 2)])
    grad_normed = gx[:rows] + swap(gx[rows:], 2) + from_later.astype(F32)
    own_normed, own_inverse = normed[:rows], inverse[:rows]
    grad_inputs = cotangent + own_inverse * (
        grad_normed
        - jnp.mean(grad_normed, axis=1, keepdims=True)
        - own_normed * jnp.mean(grad_normed * own_normed, axis=1, keepdims=True)
    )
    row = lambda t: t.reshape(1, -1)
    return (result, grad_inputs, row(grads), row(new_params), row(new_first), row(new_second))


def solution(mesh):
    rows2 = P(AX, None)
    return jax.shard_map(
        on_device,
        mesh=mesh,
        in_specs=(rows2, rows2, P(AX), P(AX), rows2, rows2, rows2),
        out_specs=(rows2,) * 6,
        check_vma=False,
    )
```

```python
import functools

import jax
import jax.numpy as jnp
from jax import lax
from jax.experimental import pallas as pl
from jax.experimental.pallas import tpu as pltpu
from jax.sharding import PartitionSpec as P

D = 768
HEADS = 12
HEAD_DIM = 64
ROT = 16
FF = 3072
HALF = D // 2
FFH = FF // 2
NVEC = 8 * D + FF
AX = ("dp", "ctx")
BF = jnp.bfloat16
F32 = jnp.float32

norm_eps = 1e-05
beta_first = 0.9
beta_second = 0.95
learn_rate = 0.01
weight_decay = 0.01
adam_eps = 1e-08
adam_steps = 3
rope_base = 10000.0
NEG = -1e30


def swap(value, mask):
    size = lax.axis_size("dp") * lax.axis_size("ctx")
    return lax.ppermute(value, AX, [(i, i ^ mask) for i in range(size)])


def pick(value, index, axis):
    return lax.dynamic_index_in_dim(value, index, axis, keepdims=False)


def gather_pair(both, rows_a, after=None):
    got = [swap(both, 8), swap(both, 16), swap(both, 24)]
    z_all = jnp.stack([both] + got)
    part_a, part_b = z_all[:, :rows_a], z_all[:, rows_a:]
    eight_a = jnp.stack([part_a, swap(part_a, 1)])
    eight_b = jnp.stack([part_b, swap(part_b, 4)])
    return (eight_a, swap(eight_a, 4), eight_b, swap(eight_b, 1)), got[2]


def whole(shape):
    return pl.BlockSpec(shape, lambda *_: (0,) * len(shape))


SMEM = pl.BlockSpec(memory_space=pltpu.SMEM)
VMEM = pl.BlockSpec(memory_space=pltpu.VMEM)
HBM = pl.BlockSpec(memory_space=pl.ANY)


def local_call(kernel, place, inputs, outs, scratch=(), in_specs=None, size=4_000_000):
    return pl.pallas_call(
        kernel,
        out_shape=[jax.ShapeDtypeStruct(shape, kind) for shape, kind in outs],
        in_specs=[SMEM] + (in_specs or [VMEM] * len(inputs)),
        out_specs=[VMEM] * len(outs),
        scratch_shapes=list(scratch),
        cost_estimate=pl.CostEstimate(flops=0, bytes_accessed=size, transcendentals=0),
    )(place, *inputs)


def copy_all(copies):
    for one in copies:
        one.start()
    for one in copies:
        one.wait()


LANES = 128
AT_DENSE, AT_UP, AT_DOWN, AT_VEC, AT_END = 432, 576, 1152, 1728, 1736
NPAR = AT_VEC * LANES + 288


def flat_to_rows(flat_ref, rows_ref):
    for k in range(AT_VEC // 8):
        rows_ref[8 * k : 8 * k + 8, :] = flat_ref[0:1, 1024 * k : 1024 * k + 1024].reshape(8, 128)


def half_tiles(tiles, core):
    lane = lax.broadcasted_iota(jnp.int32, tiles[0].shape, 1)
    roll = lambda t: pltpu.roll(t, 64, 1)
    mix = lambda first, second: jnp.where(lane < 64, first, second)
    out = []
    for k in range(4):
        t0, t1, t2, u0, u1, u2 = tiles[6 * k : 6 * k + 6]
        if core == 0:
            out += [t0, mix(t1, roll(u0)), mix(roll(u0), roll(u1))]
        else:
            out += [mix(roll(t1), roll(t2)), mix(roll(t2), u1), u2]
    return out


def full_tiles(first, second):
    lane = lax.broadcasted_iota(jnp.int32, first[0].shape, 1)
    roll = lambda t: pltpu.roll(t, 64, 1)
    mix = lambda a, b: jnp.where(lane < 64, a, b)
    out = []
    for k in range(4):
        a0, a1, a2 = first[3 * k : 3 * k + 3]
        b0, b1, b2 = second[3 * k : 3 * k + 3]
        out += [a0, mix(a1, roll(b0)), mix(roll(b0), roll(b1))]
        out += [mix(roll(a1), roll(a2)), mix(roll(a2), b1), b2]
    return out


def prep_kernel(place_ref, flat_ref, mine_ref, other_ref, down_ref, rows_ref):
    flat_to_rows(flat_ref, rows_ref)
    is_zero = place_ref[3] == 0
    base = AT_VEC * LANES
    zero = jnp.zeros((8, 128), F32)
    rows_ref[AT_VEC : AT_VEC + 8, :] = zero
    for k in range(2):
        rows_ref[AT_VEC + k : AT_VEC + k + 1, :] = flat_ref[0:1, base + 128 * k : base + 128 * k + 128]
    rows_ref[AT_VEC + 2 : AT_VEC + 3, 0:32] = flat_ref[0:1, base + 256 : base + 288]
    for b in range(3):
        span = slice(8 * b, 8 * b + 8)
        tile = lambda start, per, t: rows_ref[pl.ds(start + 8 * per * b + t, 8, stride=per), :]
        ups = [tile(AT_UP, 24, t) for t in range(24)]
        sets = []
        for c in range(2):
            tiles = [tile(0, 18, 6 * j + 3 * c + u) for j in range(3) for u in range(3)]
            tiles.append(rows_ref[AT_VEC : AT_VEC + 8, :] if b == 0 else zero)
            tiles += half_tiles(ups, c)
            tiles += [tile(AT_DENSE, 6, 3 * c + u) for u in range(3)]
            sets.append(tiles)
        for t in range(25):
            at = slice(128 * t, 128 * t + 128)
            mine_ref[span, at] = jnp.where(is_zero, sets[0][t], sets[1][t]).astype(BF)
            other_ref[span, at] = jnp.where(is_zero, sets[1][t], sets[0][t]).astype(BF)
    for b in range(12):
        for t in range(6):
            down_ref[8 * b : 8 * b + 8, 128 * t : 128 * t + 128] = rows_ref[
                pl.ds(AT_DOWN + 48 * b + t, 8, stride=6), :
            ].astype(BF)


Q_END, U_END, PACK = 1280, 2816, 3200
ROWS_A = 96


def regroup_q_kernel(place_ref, mine_ref, got_ref, q_ref):
    core = place_ref[3]
    q_ref[core] = mine_ref[:, :Q_END]
    q_ref[1 - core] = got_ref[:, :Q_END]


def regroup_ud_kernel(place_ref, mine_ref, got_ref, down_ref, after_ref, out_ref):
    del after_ref
    is_zero = place_ref[3] == 0
    for c in range(2):
        first, second = (mine_ref, got_ref) if c == 0 else (got_ref, mine_ref)
        take = lambda lo, hi: jnp.where(is_zero, first[:, lo:hi], second[:, lo:hi])
        for h in range(2):
            at = 24 * (2 * c + h)
            out_ref[at : at + 24, :] = take(Q_END + 768 * h, Q_END + 768 * h + 768)
        out_ref[192:216, 384 * c : 384 * c + 384] = take(U_END, PACK)
    out_ref[96:192, :] = down_ref[...]


def blocks_of(place_ref, a8, ay, b8, bx):
    outer_me = place_ref[2] * 2 + place_ref[1]
    for j in range(16):
        rel_z, rel_y, rel_x = j >> 2, (j >> 1) & 1, j & 1
        src_a = (ay if rel_y else a8).at[rel_x, rel_z]
        src_b = (bx if rel_x else b8).at[rel_y, rel_z]
        yield j, outer_me ^ (rel_z * 2 + rel_y), place_ref[0] ^ rel_x, src_a, src_b


def assemble_q_kernel(place_ref, a8, ay, b8, bx, out, vec_ref, up_ref, sems, lin_ref):
    copies = []
    for j, outer, xx, src_a, src_b in blocks_of(place_ref, a8, ay, b8, bx):
        copies.append(pltpu.make_async_copy(src_a, out.at[outer, 0, xx], sems.at[2 * j]))
        copies.append(pltpu.make_async_copy(src_b, out.at[outer, 1, xx], sems.at[2 * j + 1]))
    copy_all(copies)
    lin_ref[...] = jnp.zeros_like(lin_ref)
    lane = lax.broadcasted_iota(jnp.int32, (8, 128), 1)
    for r in range(32):
        block = out[r >> 2, (r >> 1) & 1, r & 1, 0:8, 3 * HALF : 3 * HALF + 128].astype(F32)
        base, shift = divmod(288 * r, 128)
        if shift:
            block = pltpu.roll(block, shift, 1)
        for k in range(3):
            line = block[k : k + 1, :]
            upper = lane[0:1, :] >= shift
            lin_ref[base + k : base + k + 1, :] += jnp.where(upper, line, 0.0)
            if shift:
                lin_ref[base + k + 1 : base + k + 2, :] += jnp.where(upper, 0.0, line)
    vec_ref[...] = jnp.zeros_like(vec_ref)
    for u in range(6):
        vec_ref[0:12, 128 * u : 128 * u + 128] = lin_ref[pl.ds(u, 12, stride=6), :]
    is_zero = place_ref[3] == 0
    tiles = [lin_ref[18 + t : 19 + t, :] for t in range(24)]
    zero, one = half_tiles(tiles, 0), half_tiles(tiles, 1)
    up_ref[...] = jnp.zeros_like(up_ref)
    for t in range(12):
        up_ref[0:1, 128 * t : 128 * t + 128] = jnp.where(is_zero, zero[t], one[t])


def assemble_ud_kernel(place_ref, a8, ay, b8, bx, up, down, dense, sems):
    copies = []
    for j, outer, xx, src_a, src_b in blocks_of(place_ref, a8, ay, b8, bx):
        for c in range(2):
            for h in range(2):
                copies.append(
                    pltpu.make_async_copy(
                        src_a.at[pl.ds(24 * (2 * c + h), 24)],
                        up.at[outer, c, xx, :, pl.ds(768 * h, 768)],
                        sems.at[6 * j + 2 * c + h],
                    )
                )
        copies.append(
            pltpu.make_async_copy(src_b.at[pl.ds(0, 96)], down.at[outer, xx], sems.at[6 * j + 4])
        )
        copies.append(
            pltpu.make_async_copy(src_b.at[pl.ds(96, 24)], dense.at[outer, xx], sems.at[6 * j + 5])
        )
    copy_all(copies)


def q_blocks(refs, part, outer, xx):
    gq, gkv, lanes = refs
    yield gq[outer, part, xx], slice(0, 24), slice(0, HALF)
    yield gkv[outer, part, xx], slice(0, 24), slice(HALF, 3 * HALF)
    yield lanes[outer, part, xx], slice(0, 24), slice(3 * HALF, Q_END)


def ud_blocks(refs, part, outer, xx, core):
    up, down, keep, got = refs
    if part == 0:
        for c in range(2):
            for h in range(2):
                at = 24 * (2 * c + h)
                yield up[outer, c, xx, :, 768 * h : 768 * h + 768], slice(at, at + 24), slice(0, 768)
    else:
        yield down[outer, xx], slice(0, 96), slice(0, 768)
        mine = lax.shift_right_logical(outer, 2) == core
        for c in range(2):
            value = jnp.where(mine, keep[outer & 3, c, xx], got[outer & 3, c, xx])
            yield value, slice(96, 120), slice(HALF * c, HALF * c + HALF)


def rs_first_kernel(blocks, count, place_ref, *refs):
    x, y, core = place_ref[0], place_ref[1], place_ref[3]
    ins, (send_a, send_b) = refs[:count], refs[count:]

    def body(i, carry):
        for value, rows, cols in blocks(ins, 0, i, 1 - x, core):
            send_a[i, rows, cols] = value.astype(BF)
        z, xx = lax.shift_right_logical(i, 1), i & 1
        for value, rows, cols in blocks(ins, 1, 2 * z + 1 - y, xx, core):
            send_b[i, rows, cols] = value.astype(BF)
        return carry

    lax.fori_loop(0, 8, body, 0)


def rs_second_kernel(blocks, count, place_ref, *refs):
    x, y, core = place_ref[0], place_ref[1], place_ref[3]
    ins, (got_a, got_b, send_a, keep_a, send_b, keep_b) = refs[:count], refs[count:]

    def body(z, carry):
        for yy, out in ((1 - y, send_a), (y, keep_a)):
            for value, rows, cols in blocks(ins, 0, 2 * z + yy, x, core):
                total = value + got_a[2 * z + yy, rows, cols].astype(F32)
                out[z, rows, cols] = total.astype(out.dtype)
        for xx, out in ((1 - x, send_b), (x, keep_b)):
            for value, rows, cols in blocks(ins, 1, 2 * z + y, xx, core):
                total = value + got_b[2 * z + xx, rows, cols].astype(F32)
                out[z, rows, cols] = total.astype(out.dtype)
        return carry

    lax.fori_loop(0, 4, body, 0)


def rs_third_kernel(place_ref, keep_a, got_a, keep_b, got_b, s1, s2, s3, own):
    z = place_ref[2]
    cut = keep_a.shape[1]
    for k, out in enumerate((own, s1, s2, s3)):
        out[:cut] = (keep_a[z ^ k] + got_a[z ^ k].astype(F32)).astype(out.dtype)
        out[cut:] = (keep_b[z ^ k] + got_b[z ^ k].astype(F32)).astype(out.dtype)


def reduce_staged(blocks, place, inputs, shape_a, shape_b):
    count = len(inputs)
    dims = lambda n, shape: (n,) + shape
    send_a, send_b = local_call(
        functools.partial(rs_first_kernel, blocks, count), place, inputs,
        [(dims(8, shape_a), BF), (dims(8, shape_b), BF)],
    )
    got = [swap(send_a, 1), swap(send_b, 4)]
    send_a, keep_a, send_b, keep_b = local_call(
        functools.partial(rs_second_kernel, blocks, count), place, inputs + got,
        [(dims(4, s), k) for s in (shape_a, shape_b) for k in (BF, F32)],
    )
    got_a, got_b = swap(send_a, 4), swap(send_b, 1)
    both = (shape_a[0] + shape_b[0], shape_a[1])
    s1, s2, s3, own = local_call(
        rs_third_kernel, place, [keep_a, got_a, keep_b, got_b],
        [(both, BF)] * 3 + [(both, F32)],
    )
    return [own, swap(s1, 8), swap(s2, 16), swap(s3, 24)]


def total_of(parts, rows, cols):
    own, g1, g2, g3 = parts
    return own[rows, cols] + g1[rows, cols].astype(F32) + g2[rows, cols].astype(F32) + g3[rows, cols].astype(F32)


def end_q_kernel(place_ref, own, g1, g2, g3, keep, send):
    core = place_ref[3]
    parts = (own, g1, g2, g3)
    keep[...] = total_of(parts, core, slice(None))
    send[...] = total_of(parts, 1 - core, slice(None))


def end_ud_kernel(place_ref, own, g1, g2, g3, keep, send, down):
    is_zero = place_ref[3] == 0
    parts = (own, g1, g2, g3)
    every = slice(0, 768)
    zero, one = total_of(parts, slice(0, 48), every), total_of(parts, slice(48, 96), every)
    keep[0:48, :] = jnp.where(is_zero, zero, one)
    send[0:48, :] = jnp.where(is_zero, one, zero)
    down[...] = total_of(parts, slice(96, 192), every)
    rest = total_of(parts, slice(192, 216), every)
    blank = jnp.zeros((24, HALF), F32)
    keep[48:72, 0:HALF] = jnp.where(is_zero, rest[:, :HALF], rest[:, HALF:])
    send[48:72, 0:HALF] = jnp.where(is_zero, rest[:, HALF:], rest[:, :HALF])
    keep[48:72, HALF:] = blank
    send[48:72, HALF:] = blank


def lanes_kernel(place_ref, sums, bdown, bup, norms, out, lin_ref):
    is_zero = place_ref[3] == 0
    zero128 = jnp.zeros((1, 128), F32)
    for u in range(6):
        at = slice(128 * (u % 3), 128 * (u % 3) + 128)
        here = is_zero if u < 3 else jnp.logical_not(is_zero)
        lin_ref[u : u + 1, :] = jnp.where(here, sums[0:1, at] + sums[8:9, at], zero128)
        lin_ref[6 + u : 7 + u, :] = jnp.where(here, sums[1:2, at] + sums[9:10, at], zero128)
        full = slice(128 * u, 128 * u + 128)
        lin_ref[12 + u : 13 + u, :] = bdown[0:1, full]
        lin_ref[42 + u : 43 + u, :] = bdown[0:1, full]
        for k in range(4):
            lin_ref[48 + 6 * k + u : 49 + 6 * k + u, :] = norms[k : k + 1, full]
    tiles = [bup[0:1, 128 * t : 128 * t + 128] for t in range(12)]
    none = [zero128] * 12
    zero, one = full_tiles(tiles, none), full_tiles(none, tiles)
    for t in range(24):
        lin_ref[18 + t : 19 + t, :] = jnp.where(is_zero, zero[t], one[t])
    lin_ref[72:80, :] = jnp.zeros((8, 128), F32)
    out[...] = jnp.zeros_like(out)
    lane = lax.broadcasted_iota(jnp.int32, (1, 128), 1)
    for r in range(32):
        base, shift = divmod(288 * r, 128)
        for k in range(3):
            line = lin_ref[base + k : base + k + 1, :]
            if shift:
                follow = lin_ref[base + k + 1 : base + k + 2, :]
                back = 128 - shift
                line = jnp.where(lane < back, pltpu.roll(line, back, 1), pltpu.roll(follow, back, 1))
            if k == 2:
                line = jnp.where(lane < 32, line, 0.0)
            out[r >> 2, (r >> 1) & 1, r & 1, k : k + 1, :] = line


def final_kernel(place_ref, q_keep, q_got, ud_keep, ud_got, down, grads, squares, rows_ref):
    is_zero = place_ref[3] == 0
    total = jnp.zeros((8, 128), F32)
    for b in range(3):
        span = slice(8 * b, 8 * b + 8)

        def halves(keep, got, rows, cols):
            k, g = keep[rows, cols], got[rows, cols]
            return jnp.where(is_zero, k, g), jnp.where(is_zero, g, k)

        def put(start, per, t, value):
            rows_ref[pl.ds(start + 8 * per * b + t, 8, stride=per), :] = value
            return value * value

        for j in range(3):
            for u in range(3):
                at = slice(128 * (3 * j + u), 128 * (3 * j + u) + 128)
                for c, value in enumerate(halves(q_keep, q_got, span, at)):
                    total += put(0, 18, 6 * j + 3 * c + u, value)
        for u in range(3):
            at = slice(128 * u, 128 * u + 128)
            for c, value in enumerate(halves(ud_keep, ud_got, slice(48 + 8 * b, 56 + 8 * b), at)):
                total += put(AT_DENSE, 6, 3 * c + u, value)
        pairs = [
            halves(ud_keep, ud_got, slice(24 * (t // 6) + 8 * b, 24 * (t // 6) + 8 * b + 8), slice(128 * (t % 6), 128 * (t % 6) + 128))
            for t in range(12)
        ]
        for t, value in enumerate(full_tiles([p[0] for p in pairs], [p[1] for p in pairs])):
            total += put(AT_UP, 24, t, value)
    for b in range(12):
        for t in range(6):
            value = down[8 * b : 8 * b + 8, 128 * t : 128 * t + 128]
            rows_ref[pl.ds(AT_DOWN + 48 * b + t, 8, stride=6), :] = value
            total += value * value
    vec = q_keep[0:8, 3 * HALF : Q_END] + q_got[0:8, 3 * HALF : Q_END]
    total += vec * vec
    squares[...] = jnp.broadcast_to(jnp.sum(total, keepdims=True), (8, 128))
    for k in range(AT_VEC // 8):
        grads[0:1, 1024 * k : 1024 * k + 1024] = rows_ref[8 * k : 8 * k + 8, :].reshape(1, 1024)
    base = AT_VEC * LANES
    for k in range(2):
        grads[0:1, base + 128 * k : base + 128 * k + 128] = vec[k : k + 1, :]
    grads[0:1, base + 256 : base + 288] = vec[2:3, 0:32]


def adam_kernel(squares, g_ref, p_ref, m_ref, v_ref, new_p, new_m, new_v):
    updated = adam_update(p_ref[...], g_ref[...], m_ref[...], v_ref[...], squares[0:1, 0:1])
    new_p[...], new_m[...], new_v[...] = updated


def run_adam(squares, grads, params, first, second):
    return pl.pallas_call(
        adam_kernel,
        in_specs=[VMEM] * 5,
        out_specs=[VMEM] * 3,
        out_shape=[jax.ShapeDtypeStruct(params.shape, F32)] * 3,
        cost_estimate=pl.CostEstimate(flops=0, bytes_accessed=6_000_000, transcendentals=0),
    )(squares, grads, params, first, second)


def rope_chunk(u, cosine, low, high):
    return u * cosine + pltpu.roll(u, 120, 1) * low + pltpu.roll(u, 8, 1) * high


def norm_rows(x_ref):
    inputs = x_ref[...].astype(F32)
    centred = inputs - jnp.mean(inputs, axis=1, keepdims=True)
    inverse = lax.rsqrt(jnp.mean(centred * centred, axis=1, keepdims=True) + norm_eps)
    return centred * inverse, inverse


def qkv_kernel(x_ref, w_ref, vec_ref, bias_ref, c_ref, lo_ref, hi_ref, q_ref, k_ref, v_ref, a1_ref, a2_ref):
    normed, _ = norm_rows(x_ref)
    a1 = (normed * vec_ref[8:9, :] + vec_ref[9:10, :]).astype(BF)
    a1_ref[...] = a1
    a2_ref[...] = (normed * vec_ref[10:11, :] + vec_ref[11:12, :]).astype(BF)
    proj = jnp.dot(a1, w_ref[:, : 3 * HALF], preferred_element_type=F32)
    cosine, low, high = c_ref[...], lo_ref[...], hi_ref[...]
    for j in range(3):
        at = slice(128 * j, 128 * j + 128)
        q = proj[:, 128 * j : 128 * j + 128] + bias_ref[0:1, at]
        q_ref[:, at] = (rope_chunk(q, cosine, low, high).astype(BF).astype(F32) * 0.125).astype(BF)
        k = proj[:, HALF + 128 * j : HALF + 128 * j + 128]
        k_ref[:, at] = rope_chunk(k, cosine, low, high).astype(BF)
    v_ref[...] = (proj[:, 2 * HALF :] + bias_ref[1:2, :]).astype(BF)


def far_kernel(used_ref, x_ref, w_ref, vec_ref, bias_ref, c_ref, lo_ref, hi_ref, k_ref, v_ref, a1_ref):
    @pl.when(used_ref[0] > 0)
    def _():
        normed, _ = norm_rows(x_ref)
        a1 = (normed * vec_ref[8:9, :] + vec_ref[9:10, :]).astype(BF)
        a1_ref[...] = a1
        proj = jnp.dot(a1, w_ref[:, HALF : 3 * HALF], preferred_element_type=F32)
        cosine, low, high = c_ref[...], lo_ref[...], hi_ref[...]
        for j in range(3):
            at = slice(128 * j, 128 * j + 128)
            k = proj[:, 128 * j : 128 * j + 128]
            k_ref[:, at] = rope_chunk(k, cosine, low, high).astype(BF)
        v_ref[...] = (proj[:, HALF:] + bias_ref[1:2, :]).astype(BF)

    @pl.when(used_ref[0] == 0)
    def _():
        k_ref[...] = jnp.zeros_like(k_ref)
        v_ref[...] = jnp.zeros_like(v_ref)
        a1_ref[...] = jnp.zeros_like(a1_ref)


def run_qkv(x, w, vecs, biases, tables, used=None):
    rows = x.shape[0]
    blk = 256
    row = lambda cols: pl.BlockSpec((blk, cols), lambda i, *_: (i, 0))
    specs = [row(D), whole(w.shape), whole(vecs.shape), whole(biases.shape)] + [row(128)] * 3
    wide = lambda cols: jax.ShapeDtypeStruct((rows, cols), BF)
    cost = pl.CostEstimate(flops=2 * rows * D * 3 * HALF, bytes_accessed=8_000_000, transcendentals=0)
    if used is None:
        return pl.pallas_call(
            qkv_kernel,
            grid=(rows // blk,),
            in_specs=specs,
            out_specs=[row(HALF)] * 3 + [row(D)] * 2,
            out_shape=[wide(HALF)] * 3 + [wide(D)] * 2,
            cost_estimate=cost,
        )(x, w, vecs, biases, *tables)
    return pl.pallas_call(
        far_kernel,
        grid_spec=pltpu.PrefetchScalarGridSpec(
            num_scalar_prefetch=1,
            grid=(rows // blk,),
            in_specs=specs,
            out_specs=[row(HALF)] * 2 + [row(D)],
        ),
        out_shape=[wide(HALF)] * 2 + [wide(D)],
        cost_estimate=cost,
    )(used, x, w, vecs, biases, *tables)


QB = 256


def variants(rows):
    cases = []
    for qb in range(rows // QB):
        for near in range(qb + 1):
            if near == 0:
                cases += [(qb, 0, far) for far in range(rows // QB + 1)]
            else:
                cases.append((qb, near, 0))
    return cases


def load_keys(far_ref, near_ref, rows, qb, near, far):
    parts = []
    if far:
        parts.append(far_ref[rows - far * QB : rows, :])
    parts.append(near_ref[near * QB : (qb + 1) * QB, :])
    return parts[0] if len(parts) == 1 else jnp.concatenate(parts, axis=0)


def attn_fwd_kernel(rows, plan_ref, q_ref, k_ref, v_ref, kf_ref, vf_ref, start_ref, o_ref, lse_ref):
    seq = pl.program_id(0)
    lane = lax.broadcasted_iota(jnp.int32, (QB, 128), 1)
    blocks = rows // QB
    for qb, near, far in variants(rows):
        low = plan_ref[seq * blocks + qb]
        match = low == (near if far == 0 else -far)

        @pl.when(match)
        def _(qb=qb, near=near, far=far):
            keys = load_keys(kf_ref, k_ref, rows, qb, near, far)
            values = load_keys(vf_ref, v_ref, rows, qb, near, far)
            count = keys.shape[0]
            first = near * QB - far * QB
            q = q_ref[qb * QB : (qb + 1) * QB, :]
            start = start_ref[qb * QB : (qb + 1) * QB, :]
            key_at = lax.broadcasted_iota(jnp.int32, (QB, count), 1) + first
            query_at = lax.broadcasted_iota(jnp.int32, (QB, count), 0) + qb * QB
            ok = (key_at >= start) & (key_at <= query_at)
            outs, lses = [], []
            for head in range(2):
                mine = (lane < 64) if head == 0 else (lane >= 64)
                qh = jnp.where(mine, q, jnp.zeros_like(q))
                s = lax.dot_general(qh, keys, (((1,), (1,)), ((), ())), preferred_element_type=F32)
                s = jnp.where(ok, s, NEG)
                top = jnp.max(s, axis=1, keepdims=True)
                e = jnp.exp(s - top)
                total = jnp.sum(e, axis=1, keepdims=True)
                prob = (e * (1.0 / total)).astype(BF)
                outs.append(jnp.dot(prob, values, preferred_element_type=F32))
                lses.append(jnp.broadcast_to(top + jnp.log(total), (QB, 128)))
            o_ref[qb * QB : (qb + 1) * QB, :] = jnp.where(lane < 64, outs[0], outs[1]).astype(BF)
            lse_ref[qb * QB : (qb + 1) * QB, :] = jnp.where(lane < 64, lses[0], lses[1])


def attn_bwd_kernel(
    rows, plan_ref, q_ref, k_ref, v_ref, kf_ref, vf_ref, start_ref, o_ref, do_ref, lse_ref,
    c_ref, lo_ref, hi_ref, cf_ref, lof_ref, hif_ref,
    dq_ref, dk_ref, dv_ref, dkf_ref, dvf_ref, sum_ref, dk_acc, dv_acc, lse_t, delta_t, start_t,
):
    seq = pl.program_id(0)
    blocks = rows // QB
    lane = lax.broadcasted_iota(jnp.int32, (QB, 128), 1)
    sub = lax.broadcasted_iota(jnp.int32, (128, QB), 0)
    dk_acc[...] = jnp.zeros_like(dk_acc)
    dv_acc[...] = jnp.zeros_like(dv_acc)
    lse_t[...] = jnp.transpose(lse_ref[...])
    delta_t[...] = jnp.transpose(do_ref[...].astype(F32) * o_ref[...].astype(F32))
    start_t[...] = jnp.transpose(jnp.broadcast_to(start_ref[...], (rows, 128)).astype(F32))[0:8, :]
    for qb, near, far in variants(rows):
        low = plan_ref[seq * blocks + qb]
        match = low == (near if far == 0 else -far)

        @pl.when(match)
        def _(qb=qb, near=near, far=far):
            keys = load_keys(kf_ref, k_ref, rows, qb, near, far)
            values = load_keys(vf_ref, v_ref, rows, qb, near, far)
            count = keys.shape[0]
            first = near * QB - far * QB
            at = slice(qb * QB, (qb + 1) * QB)
            q, do = q_ref[at, :], do_ref[at, :]
            start = start_t[0:1, at]
            key_at = lax.broadcasted_iota(jnp.int32, (count, QB), 0) + first
            query_at = lax.broadcasted_iota(jnp.int32, (count, QB), 1) + qb * QB
            ok = (key_at >= start.astype(jnp.int32)) & (key_at <= query_at)
            keys_t = jnp.transpose(keys)
            dqs, dk, dv = [], None, None
            for head in range(2):
                mine = (lane < 64) if head == 0 else (lane >= 64)
                hs = slice(64 * head, 64 * head + 64)
                qh = jnp.where(mine, q, jnp.zeros_like(q))
                doh = jnp.where(mine, do, jnp.zeros_like(do))
                lse = lse_t[64 * head : 64 * head + 1, at]
                delta = jnp.sum(delta_t[hs, at], axis=0, keepdims=True)
                nt = (((1,), (1,)), ((), ()))
                s = lax.dot_general(keys, qh, nt, preferred_element_type=F32)
                prob = jnp.where(ok, jnp.exp(s - lse), 0.0)
                dprob = lax.dot_general(values, doh, nt, preferred_element_type=F32)
                ds = (prob * (dprob - delta)).astype(BF)
                dv_h = jnp.dot(prob.astype(BF), doh, preferred_element_type=F32)
                dk_h = jnp.dot(ds, qh, preferred_element_type=F32)
                dv = dv_h if dv is None else dv + dv_h
                dk = dk_h if dk is None else dk + dk_h
                dqs.append(jnp.dot(keys_t, ds, preferred_element_type=F32))
            dq = jnp.transpose(jnp.where(sub < 64, dqs[0], dqs[1])) * 0.125
            dq = rope_chunk(dq, c_ref[at, :], -lo_ref[at, :], -hi_ref[at, :])
            dq_ref[at, :] = dq.astype(BF)
            part = jnp.sum(dq, axis=0, keepdims=True)
            if qb == 0:
                sum_ref[0:1, :] = part
            else:
                sum_ref[0:1, :] += part
            span = slice(rows + first, rows + first + count)
            dk_acc[span, :] += dk
            dv_acc[span, :] += dv
    dk_ref[...] = rope_chunk(dk_acc[rows:, :], c_ref[...], -lo_ref[...], -hi_ref[...]).astype(BF)
    dkf_ref[...] = rope_chunk(dk_acc[:rows, :], cf_ref[...], -lof_ref[...], -hif_ref[...]).astype(BF)
    dv_ref[...] = dv_acc[rows:, :].astype(BF)
    dvf_ref[...] = dv_acc[:rows, :].astype(BF)
    sum_ref[1:2, :] = jnp.sum(dv_acc[...], axis=0, keepdims=True)
    sum_ref[2:8, :] = jnp.zeros((6, 128), F32)


def attn_specs(rows):
    block = pl.BlockSpec((rows, 128), lambda s, p, *_: (s, p))
    per_seq = lambda cols: pl.BlockSpec((rows, cols), lambda s, p, *_: (s, 0))
    return block, per_seq


def attn_fwd(plan, q, k, v, kf, vf, start):
    total = q.shape[0]
    rows = total // 2
    block, per_seq = attn_specs(rows)
    return pl.pallas_call(
        functools.partial(attn_fwd_kernel, rows),
        grid_spec=pltpu.PrefetchScalarGridSpec(
            num_scalar_prefetch=1,
            grid=(2, HALF // 128),
            in_specs=[block] * 5 + [per_seq(1)],
            out_specs=[block] * 2,
        ),
        out_shape=[
            jax.ShapeDtypeStruct((total, HALF), BF),
            jax.ShapeDtypeStruct((total, HALF), F32),
        ],
        cost_estimate=pl.CostEstimate(
            flops=20_000_000_000, bytes_accessed=6_000_000, transcendentals=0
        ),
    )(plan, q, k, v, kf, vf, start)


def attn_bwd(plan, q, k, v, kf, vf, start, o, do, lse, tables, tables_far):
    total = q.shape[0]
    rows = total // 2
    block, per_seq = attn_specs(rows)
    wide = jax.ShapeDtypeStruct((total, HALF), BF)
    return pl.pallas_call(
        functools.partial(attn_bwd_kernel, rows),
        grid_spec=pltpu.PrefetchScalarGridSpec(
            num_scalar_prefetch=1,
            grid=(2, HALF // 128),
            in_specs=[block] * 5 + [per_seq(1)] + [block] * 3 + [per_seq(128)] * 6,
            out_specs=[block] * 5 + [pl.BlockSpec((8, 128), lambda s, p, *_: (s, p))],
            scratch_shapes=[pltpu.VMEM((2 * rows, 128), F32)] * 2
            + [pltpu.VMEM((128, rows), F32)] * 2
            + [pltpu.VMEM((8, rows), F32)],
        ),
        out_shape=[wide] * 5 + [jax.ShapeDtypeStruct((16, HALF), F32)],
        cost_estimate=pl.CostEstimate(
            flops=40_000_000_000, bytes_accessed=10_000_000, transcendentals=0
        ),
    )(plan, q, k, v, kf, vf, start, o, do, lse, *tables, *tables_far)


def rotary_tables(positions):
    halfway = ROT // 2
    frequency = jnp.power(rope_base, -jnp.arange(halfway, dtype=F32) * (2.0 / ROT))
    lane = jnp.arange(128) % HEAD_DIM
    angles = positions.astype(F32)[:, None] * frequency[lane % halfway][None, :]
    sine = jnp.sin(angles)
    cosine = jnp.where(lane < ROT, jnp.cos(angles), 1.0)
    low = jnp.where(lane < halfway, -sine, 0.0)
    high = jnp.where((lane >= halfway) & (lane < ROT), sine, 0.0)
    return cosine, low, high


def gelu_exact(inputs):
    return 0.5 * inputs * (1.0 + lax.erf(inputs * 0.7071067811865476))


def gelu_slope(inputs):
    return (
        0.5 * (1.0 + lax.erf(inputs * 0.7071067811865476))
        + inputs * jnp.exp(-0.5 * inputs * inputs) * 0.3989422804014327
    )


def normalize(inputs):
    centred = inputs - jnp.mean(inputs, axis=1, keepdims=True)
    inverse = lax.rsqrt(jnp.mean(centred * centred, axis=1, keepdims=True) + norm_eps)
    return (centred * inverse, inverse)


def adam_update(params, grads, first_moment, second_moment, squares_total):
    clip_factor = jnp.minimum(1.0, 1.0 / jnp.sqrt(squares_total + 1e-12))
    clipped = grads * clip_factor
    new_first = beta_first * first_moment + (1.0 - beta_first) * clipped
    new_second = beta_second * second_moment + (1.0 - beta_second) * clipped * clipped
    corrected_first = new_first / (1.0 - beta_first**adam_steps)
    corrected_second = new_second / (1.0 - beta_second**adam_steps)
    new_params = params - learn_rate * (
        corrected_first / (jnp.sqrt(corrected_second) + adam_eps) + weight_decay * params
    )
    return (new_params, new_first, new_second)


def split_shard(flat, owners):
    pieces, offset = [], 0
    for height, breadth in ((D, 3 * D), (D, D), (D, FF), (FF, D)):
        extent = height // owners * breadth
        pieces.append(flat[offset : offset + extent].reshape(height // owners, breadth))
        offset += extent
    pieces.append(flat[offset:])
    return pieces


def on_device(tokens, out_grad, segments, positions, params, first_moment, second_moment):
    owners = lax.axis_size("dp") * lax.axis_size("ctx")
    staged = owners == 32
    me = (lax.axis_index("dp") * lax.axis_size("ctx") + lax.axis_index("ctx")).astype(jnp.int32)
    ctx, core = me & 1, (me >> 1) & 1
    place = jnp.stack([ctx, (me >> 2) & 1, me >> 3, core])
    is_zero = core == 0
    rows = tokens.shape[0]
    group = 2 * (FF // owners)

    if staged:
        mine, other, own_rows = local_call(
            prep_kernel, place, [params],
            [((24, PACK), BF), ((24, PACK), BF), ((96, D), BF)],
            scratch=[pltpu.VMEM((AT_END, LANES), F32)],
        )
        got = swap(other, 2)
        q_pair = local_call(regroup_q_kernel, place, [mine, got], [((2, 24, Q_END), BF)])[0]
        q_pieces, after = gather_pair(q_pair, 1)
        ud_block = local_call(
            regroup_ud_kernel, place, [mine, got, own_rows, after], [((216, D), BF)],
            in_specs=[VMEM] * 3 + [HBM],
        )[0]
        ud_pieces, _ = gather_pair(ud_block, ROWS_A)
        w_q5, vecs, bias_up_half = local_call(
            assemble_q_kernel, place, [p.reshape(p.shape[:2] + p.shape[-2:]) for p in q_pieces],
            [((8, 2, 2, 24, Q_END), BF), ((16, D), F32), ((8, FFH), F32)],
            scratch=[pltpu.SemaphoreType.DMA((32,)), pltpu.VMEM((80, 128), F32)],
            in_specs=[HBM] * 4,
        )
        bias_up_half = bias_up_half[0]
        w_u5, w_d4, dense5 = local_call(
            assemble_ud_kernel, place, list(ud_pieces),
            [((8, 2, 2, 24, FFH), BF), ((8, 2, 96, D), BF), ((8, 2, 24, D), BF)],
            scratch=[pltpu.SemaphoreType.DMA((96,))],
            in_specs=[HBM] * 4,
        )
        w_q = w_q5.reshape(D, Q_END)
        w_up = w_u5.reshape(D, FFH)
        w_down = w_d4.reshape(FFH, D)
        dense_mine = dense5.reshape(8, 2, 24, 2, HALF).transpose(0, 3, 1, 2, 4).reshape(D, HALF)
        dense_got = swap(dense_mine, 2)
        w_dense = jnp.where(
            is_zero,
            jnp.concatenate([dense_mine, dense_got], axis=1),
            jnp.concatenate([dense_got, dense_mine], axis=1),
        )
    else:
        shards = split_shard(params.reshape(-1).astype(BF), owners)
        full = [lax.all_gather(p, AX, axis=0, tiled=True) for p in shards]
        w_q = pick(full[0].reshape(D, 3, 2, HALF), core, 2).reshape(D, 3 * HALF)
        w_dense = full[1]
        w_up = pick(full[2].reshape(D, FFH // group, 2, group), core, 2).reshape(D, FFH)
        w_down = pick(full[3].reshape(FFH // group, 2, group, D), core, 1).reshape(FFH, D)
        vecs = jnp.pad(full[4].astype(F32).reshape(12, D), ((0, 4), (0, 0)))
        bias_up_half = pick(vecs[3:7].reshape(FFH // group, 2, group), core, 1).reshape(FFH)
    half_of = lambda v: jnp.where(is_zero, v[:HALF], v[HALF:])
    dense_rows = lax.dynamic_slice_in_dim(w_dense, core * HALF, HALF, 0)
    biases = jnp.stack([half_of(vecs[0]), half_of(vecs[1])] + [jnp.zeros((HALF,), F32)] * 6)
    gain_one, gain_two = vecs[8], vecs[10]

    far_own = lax.ppermute(tokens, AX, [(i, i + 1) for i in range(0, owners, 2)])
    tokens_other = swap(tokens, 2)
    grad_other = swap(out_grad, 2)
    positions_all = jnp.concatenate([positions, swap(positions, 2)])
    x_all = jnp.concatenate([tokens, tokens_other], axis=0)
    g_all = jnp.concatenate([out_grad, grad_other], axis=0)
    x_far = jnp.concatenate([far_own, swap(far_own, 2)], axis=0)
    local = jnp.arange(rows, dtype=jnp.int32)
    start = (jnp.concatenate([local, local]) - positions_all)[:, None]
    heads_pos = positions_all.reshape(2, rows)[:, :1]
    far_positions = jnp.maximum(heads_pos - rows + local[None, :], 0).reshape(-1)
    tables = rotary_tables(positions_all)
    tables_far = rotary_tables(far_positions)
    least = jnp.min(start.reshape(-1, QB), axis=1)
    plan = jnp.where(least < 0, -((QB - 1 - least) // QB), least // QB)
    used = ctx.reshape(1)

    q, k, v, a1, a2 = run_qkv(x_all, w_q, vecs, biases, tables)
    kf, vf, a1f = run_qkv(x_far, w_q, vecs, biases, tables_far, used)
    att, lse = attn_fwd(plan, q, k, v, kf, vf, start)

    pre = jnp.dot(a2, w_up, preferred_element_type=F32) + bias_up_half
    act = gelu_exact(pre).astype(BF)
    grad_down = jnp.dot(act.T, g_all, preferred_element_type=F32)
    grad_pre = jnp.dot(g_all, w_down.T, preferred_element_type=F32) * gelu_slope(pre)
    grad_pre_low = grad_pre.astype(BF)
    grad_bias_up = jnp.sum(grad_pre, axis=0)
    grad_up = jnp.dot(a2.T, grad_pre_low, preferred_element_type=F32)
    g_keep = jnp.where(is_zero, g_all[:, :HALF], g_all[:, HALF:])
    g_send = jnp.where(is_zero, g_all[:, HALF:], g_all[:, :HALF])
    dense_keep = jnp.dot(att.T, g_keep, preferred_element_type=F32)
    dense_send = jnp.dot(att.T, g_send, preferred_element_type=F32)

    if staged:
        quarter = (4, 2, 2, 24, HALF)
        ud_sums = reduce_staged(
            ud_blocks, place,
            [
                grad_up.reshape(8, 2, 2, 24, FFH),
                grad_down.reshape(8, 2, 96, D),
                dense_keep.reshape(quarter),
                swap(dense_send, 2).reshape(quarter),
            ],
            (ROWS_A, D), (216 - ROWS_A, D),
        )
        ud_keep, ud_send, own_down = local_call(
            end_ud_kernel, place, ud_sums, [((72, D), F32), ((72, D), F32), ((96, D), F32)]
        )
        ud_got = swap(ud_send, 2)

    grad_att = jnp.dot(g_all, dense_rows.T, preferred_element_type=F32).astype(BF)
    gq, gk, gv, gkf, gvf, sums = attn_bwd(
        plan, q, k, v, kf, vf, start, att, grad_att, lse, tables, tables_far
    )
    gkv = jnp.concatenate([gk, gv], axis=1)
    gkvf = jnp.concatenate([gkf, gvf], axis=1)
    grad_q_cols = jnp.dot(a1.T, gq, preferred_element_type=F32)
    grad_kv_cols = jnp.dot(a1.T, gkv, preferred_element_type=F32) + jnp.dot(
        a1f.T, gkvf, preferred_element_type=F32
    )

    normed, inverse = normalize(x_all.astype(F32))
    normed_far, _ = normalize(x_far.astype(F32))
    w_qkv = w_q[:, : 3 * HALF]
    ga1 = jnp.dot(gq, w_qkv[:, :HALF].T, preferred_element_type=F32) + jnp.dot(
        gkv, w_qkv[:, HALF:].T, preferred_element_type=F32
    )
    ga1f = jnp.dot(gkvf, w_qkv[:, HALF:].T, preferred_element_type=F32)
    ga2 = jnp.dot(grad_pre_low, w_up.T, preferred_element_type=F32)
    norm_grads = [
        jnp.sum(ga1 * normed, axis=0) + jnp.sum(ga1f * normed_far, axis=0),
        jnp.sum(ga1, axis=0) + jnp.sum(ga1f, axis=0),
        jnp.sum(ga2 * normed, axis=0),
        jnp.sum(ga2, axis=0),
    ]
    cotangent = out_grad.astype(F32)
    grad_bias_out = jnp.sum(cotangent, axis=0)

    if staged:
        lanes = local_call(
            lanes_kernel, place,
            [sums, grad_bias_out[None], grad_bias_up[None], jnp.stack(norm_grads)],
            [((8, 2, 2, 24, 128), F32)],
            scratch=[pltpu.VMEM((80, 128), F32)],
        )[0]
        q_sums = reduce_staged(
            lambda refs, part, outer, xx, _: q_blocks(refs, part, outer, xx), place,
            [
                grad_q_cols.reshape(8, 2, 2, 24, HALF),
                grad_kv_cols.reshape(8, 2, 2, 24, D),
                lanes,
            ],
            (24, Q_END), (24, Q_END),
        )
        q_sums = [t.reshape(2, 24, Q_END) for t in q_sums]
        q_keep, q_send = local_call(end_q_kernel, place, q_sums, [((24, Q_END), F32)] * 2)
        grads, squares = local_call(
            final_kernel, place, [q_keep, swap(q_send, 2), ud_keep, ud_got, own_down],
            [((1, NPAR), F32), ((8, 128), F32)],
            scratch=[pltpu.VMEM((AT_END, LANES), F32)],
        )
    else:
        sums = jnp.sum(sums.reshape(2, 8, HALF), axis=0)
        nothing = jnp.zeros((HALF,), F32)
        spread = lambda t: jnp.where(
            is_zero, jnp.concatenate([t, nothing]), jnp.concatenate([nothing, t])
        )
        widen = lambda t, axis: lax.dynamic_update_slice_in_dim(
            jnp.zeros(t.shape[:axis] + (2,) + t.shape[axis + 1 :], F32), t, core, axis
        )
        grad_vector = jnp.concatenate(
            [
                spread(sums[0]),
                spread(sums[1]),
                grad_bias_out,
                widen(grad_bias_up.reshape(FFH // group, 1, group), 1).reshape(FF),
                grad_bias_out,
                *norm_grads,
            ]
        )
        scatter = lambda t: lax.psum_scatter(t, AX, scatter_dimension=0, tiled=True)
        grad_qkv = jnp.concatenate([grad_q_cols, grad_kv_cols], axis=1)
        dense_both = jnp.where(
            is_zero,
            jnp.concatenate([dense_keep, dense_send], axis=1),
            jnp.concatenate([dense_send, dense_keep], axis=1),
        )
        pieces = [
            scatter(widen(grad_qkv.reshape(D, 3, 1, HALF), 2).reshape(D, 3 * D)),
            scatter(widen(dense_both.reshape(1, HALF, D), 0).reshape(D, D)),
            scatter(widen(grad_up.reshape(D, FFH // group, 1, group), 2).reshape(D, FF)),
            scatter(widen(grad_down.reshape(FFH // group, 1, group, D), 1).reshape(FF, D)),
            scatter(grad_vector),
        ]
        grads = jnp.concatenate([t.reshape(1, -1) for t in pieces], axis=1)
        squares = jnp.broadcast_to(jnp.sum(grads * grads), (8, 128))

    bit = 1
    while bit < owners:
        squares = squares + swap(squares, bit)
        bit *= 2
    new_params, new_first, new_second = run_adam(
        squares, grads, params, first_moment, second_moment
    )

    partial_result = jnp.dot(att, dense_rows, preferred_element_type=F32) + jnp.dot(
        act, w_down, preferred_element_type=F32
    )
    result = (
        tokens.astype(F32)
        + partial_result[:rows]
        + swap(partial_result[rows:], 2)
        + (vecs[2] + vecs[7])
    ).astype(BF)
    gx = ga1 * gain_one + ga2 * gain_two
    gx_far = ga1f * gain_one
    far_total = gx_far[:rows] + swap(gx_far[rows:], 2)
    from_later = lax.ppermute(far_total.astype(BF), AX, [(i + 1, i) for i in range(0, owners, 2)])
    grad_normed = gx[:rows] + swap(gx[rows:], 2) + from_later.astype(F32)
    own_normed, own_inverse = normed[:rows], inverse[:rows]
    grad_inputs = cotangent + own_inverse * (
        grad_normed
        - jnp.mean(grad_normed, axis=1, keepdims=True)
        - own_normed * jnp.mean(grad_normed * own_normed, axis=1, keepdims=True)
    )
    return (result, grad_inputs, grads, new_params, new_first, new_second)


def solution(mesh):
    rows2 = P(AX, None)
    return jax.shard_map(
        on_device,
        mesh=mesh,
        in_specs=(rows2, rows2, P(AX), P(AX), rows2, rows2, rows2),
        out_specs=(rows2,) * 6,
        check_vma=False,
    )
```
